256 devices in a mesh: ctx: 16 (over z_hi, y, core), ep: 16 (over x, z_lo).
Axes of the slice: x: 4, y: 4, z: 8 (z_hi: 2, z_lo: 4; z = z_hi * 4 + z_lo), core: 2. Of those that a mesh axis runs over, the one named last changes fastest.
Arguments:
- queries: bfloat16 [4096, 1, 4096], P('ctx', None, 'ep'), may hold values from -6 to 6
- keys_in: bfloat16 [4096, 1, 4096], P('ctx', None, 'ep'), may hold values from -6 to 6
- values_in: bfloat16 [4096, 1, 4096], P('ctx', None, 'ep'), may hold values from -6 to 6
- log_decay: float32 [32, 1, 4096], P('ep', None, 'ctx'), may hold values from -1.5 to 0
- attn_gain: float32 [4096], P('ep'), may hold values from 0.1 to 1.9
- out_weight: bfloat16 [4096, 6144], P('ep', 'ctx'), may hold values from -0.09375 to 0.09375
- residual: bfloat16 [4096, 1, 6144], P(('ctx', 'ep')), may hold values from -42 to 42
- moe_gain: float32 [6144], replicated, may hold values from 0.1 to 1.9
- router: bfloat16 [6144, 16], replicated, may hold values from -0.078125 to 0.078125
- gate_weight: bfloat16 [16, 6144, 4608], P('ep', None, 'ctx'), may hold values from -0.078125 to 0.078125
- up_weight: bfloat16 [16, 6144, 4608], P('ep', None, 'ctx'), may hold values from -0.078125 to 0.078125
- down_weight: bfloat16 [16, 4608, 6144], P('ep', 'ctx'), may hold values from -0.09375 to 0.09375
- routes: int32 [4096, 1, 2], P(('ctx', 'ep')), may hold values from 0 to 15, all different within a row; in each aligned block of 16 rows (0 to 15, 16 to 31, ..., all dimensions but the last counted through in order) at most 3 rows name the same one
Outputs:
- mixed: bfloat16 [4096, 1, 6144], P(('ctx', 'ep'))
The draws below stay inside these ranges and needn't reach their ends.
Inputs may be any that keep to these rules, and one draw needn't show every extreme that they name: `routes`: each row names two different experts. Among the tokens of one device (aligned blocks of 16 rows of the flattened positions and sequences) no expert is named more than 3 times.
All inputs are finite; a program needn't handle non-finite values.
Results may differ from the reference program's by a relative error of at most 0.017.
Values may be sent and summed in bfloat16 or wider, within the bound.
A program may use at most 128 MiB of HBM per device.

```python
import math
import jax
import jax.numpy as jnp
import numpy as np
from jax import lax

D = 6144
HD = 128
HEADS_DEV = 2
FF = 4608
SPAN = 256
SEQUENCE_COUNT = 1
HEAD_TOTAL = 32
EXPERTS = 16
SEQUENCE_LENGTH = 4096
ROWS = 16
CAP = 3
N_CTX = 16
N_EP = 16


def draw_log_decay(key, part):
    sequence_streams = jax.random.split(key, 7)
    fast_share = 0.5
    quick = jax.random.bernoulli(sequence_streams[0], fast_share, (HEAD_TOTAL, 1, 1))
    fast_rate = jnp.exp(jax.random.uniform(sequence_streams[1], (HEAD_TOTAL, 1, 1), jnp.float32, jnp.log(1.0 / 50.0), jnp.log(1.0 / 30.0)))
    slow_rate = jax.random.uniform(sequence_streams[2], (HEAD_TOTAL, 1, 1), jnp.float32, 0.05, 0.2) / SEQUENCE_LENGTH
    baseline_rate = jnp.where(quick, fast_rate, slow_rate)
    blocks = SEQUENCE_LENGTH // SPAN
    block_multiplier = jnp.exp(jax.random.uniform(sequence_streams[3], (HEAD_TOTAL, SEQUENCE_COUNT, blocks, 1), jnp.float32, jnp.log(0.5), jnp.log(2.0)))
    block_multiplier = jnp.broadcast_to(block_multiplier, (HEAD_TOTAL, SEQUENCE_COUNT, blocks, SPAN)).reshape(HEAD_TOTAL, SEQUENCE_COUNT, SEQUENCE_LENGTH)
    jitter_level = jax.random.uniform(sequence_streams[4], (HEAD_TOTAL, SEQUENCE_COUNT, SEQUENCE_LENGTH), jnp.float32, 0.5, 1.5)
    spike_position = jax.random.randint(sequence_streams[5], (HEAD_TOTAL, SEQUENCE_COUNT, 2, 1), 0, SEQUENCE_LENGTH)
    token_position = jnp.arange(SEQUENCE_LENGTH, dtype=jnp.int32)[None, None, None, :]
    spike_events = jnp.sum((token_position == spike_position).astype(jnp.float32), axis=2)
    spike_depth = jax.random.uniform(sequence_streams[6], (HEAD_TOTAL, SEQUENCE_COUNT, SEQUENCE_LENGTH), jnp.float32, 0.22, 0.69)
    return -(baseline_rate * block_multiplier * jitter_level) - spike_events * spike_depth


def draw_residual(key, part):
    sequence_streams = jax.random.split(key, 1)
    drawn = jnp.clip(jax.random.normal(sequence_streams[0], (SEQUENCE_LENGTH, SEQUENCE_COUNT, D), jnp.float32), -6.0, 6.0)
    return drawn.astype(jnp.bfloat16)


def level_of(own_key, dims, shards, low, largest):
    def one(position, parts):
        steps = jax.random.uniform(jax.random.fold_in(jax.random.fold_in(own_key, 6), position), (parts,), jnp.float32, low / len(shards), largest / len(shards))
        return jnp.repeat(jnp.exp(steps), dims[position] // parts).reshape((-1,) + (1,) * (len(dims) - position - 1))

    level = one(*shards[0])
    for cut in shards[1:]:
        level = level * one(*cut)
    return level


def assign_block(own_key, own, number, rows, number_of, top, limit, skew):
    sequence = jax.random.permutation(own_key, number_of)
    heavy_load, common = shares(number_of, rows * top, limit, skew, True), shares(number_of, rows * top, limit, skew, False)
    places = jnp.arange(number_of)

    def named(lengths, turn):
        used = int((lengths > 0).sum())
        fixed = max(1, used // 4)
        moved = fixed + (places - fixed + turn * (used - fixed)) % max(1, number_of - fixed)
        return jnp.zeros((number_of,), jnp.int32).at[sequence[jnp.where(places < fixed, places, moved)]].set(jnp.asarray(lengths, jnp.int32))

    lengths = jnp.where(number % 4 == 0, named(heavy_load, number // 4), named(common, number - number // 4 - 1))
    mixed = jax.random.permutation(jax.random.fold_in(own, 3), number_of)
    donor, sink = mixed[0:number_of // 2 * 2:2], mixed[1:number_of // 2 * 2:2]
    margin = jnp.minimum(lengths[donor] - 1, limit - lengths[sink]) // 2
    margin = jnp.where((donor == sequence[0]) | (sink == sequence[0]) | (lengths[sink] == 0), 0, jnp.maximum(margin, 0))
    moved = jax.random.randint(jax.random.fold_in(own, 4), (number_of // 2,), 0, 1 << 20) % (margin + 1)
    lengths = lengths.at[donor].add(-moved).at[sink].add(moved)
    items = jnp.searchsorted(jnp.cumsum(lengths), jnp.arange(rows * top), side="right").astype(jnp.int32)
    table = items.reshape(top, rows).T
    table = table[jax.random.permutation(jax.random.fold_in(own, 1), rows)]
    turn = jax.random.randint(jax.random.fold_in(own, 2), (rows, 1), 0, top)
    return jnp.take_along_axis(table, (jnp.arange(top)[None, :] + turn) % top, axis=1)


def shares(count, total, most, lean, full):
    weights = [(1 << 20) // math.isqrt(standing ** lean) + 1 for standing in range(1, count + 1)]
    largest = most if full else min(most, max(-(-total // count), total * weights[0] // sum(weights)))
    least = 1 if total - largest >= count - 1 else 0
    counts, surplus = [largest] + [least] * (count - 1), total - largest - least * (count - 1)
    while surplus > 0:
        free = [i for i in range(1, count) if counts[i] < largest] or [i for i in range(1, count) if counts[i] < most]
        pool, left = sum([weights[i] for i in free]), surplus
        for i in free:
            addition = min(most - counts[i], max(1, left * weights[i] // pool), surplus)
            counts[i] = counts[i] + addition
            surplus = surplus - addition
    return np.array(counts)


def scatter_about(key, extent, scale, bound, cuts=(), kind=jnp.bfloat16):
    factor_of = level_of(key, extent, cuts, -0.22, 0.18) if cuts else 1.0
    values = jax.random.normal(key, extent, jnp.float32) * scale * factor_of
    return jnp.minimum(jnp.maximum(values, -bound), bound).astype(kind)


def setup_inputs(seed: int = 0) -> dict:
    keys = jax.random.split(jax.random.key(seed), 14)
    queries = scatter_about(keys[0], (SEQUENCE_LENGTH, SEQUENCE_COUNT, HEAD_TOTAL * HD), 1.0, 6.0, ((0, 16), (2, 16)))
    keys_in = scatter_about(keys[1], (SEQUENCE_LENGTH, SEQUENCE_COUNT, HEAD_TOTAL * HD), 1.0, 6.0, ((0, 16), (2, 16)))
    values_in = scatter_about(keys[2], (SEQUENCE_LENGTH, SEQUENCE_COUNT, HEAD_TOTAL * HD), 1.0, 6.0, ((0, 16), (2, 16)))
    log_decay = draw_log_decay(jax.random.fold_in(keys[13], 71), 0)
    attn_gain = jnp.clip(1.0 + 0.18 * jax.random.normal(keys[4], (HEAD_TOTAL * HD,), jnp.float32), 0.1, 1.9)
    out_weight = scatter_about(keys[5], (HEAD_TOTAL * HD, D), (HEAD_TOTAL * HD) ** -0.5, 0.09375, ((0, 16), (1, 16)))
    residual = draw_residual(jax.random.fold_in(keys[13], 71), 0)
    moe_gain = jnp.clip(1.0 + 0.18 * jax.random.normal(keys[7], (D,), jnp.float32), 0.1, 1.9)
    router = scatter_about(keys[8], (D, EXPERTS), D ** -0.5, 0.078125)
    gate_weight = scatter_about(keys[9], (EXPERTS, D, FF), D ** -0.5, 0.078125, ((0, 16), (2, 16)))
    up_weight = scatter_about(keys[10], (EXPERTS, D, FF), D ** -0.5, 0.078125, ((0, 16), (2, 16)))
    down_weight = scatter_about(keys[11], (EXPERTS, FF, D), FF ** -0.5, 0.09375, ((0, 16), (1, 16)))
    routes_keys = jax.random.split(jax.random.fold_in(keys[12], 1), SEQUENCE_LENGTH * SEQUENCE_COUNT // ROWS)
    routes_turns = jax.random.permutation(jax.random.fold_in(keys[12], 3), SEQUENCE_LENGTH * SEQUENCE_COUNT // ROWS)
    routes = jax.vmap(lambda own, number: assign_block(jax.random.fold_in(keys[12], 2), own, number, ROWS, EXPERTS, 2, CAP, 1))(routes_keys, routes_turns).reshape((SEQUENCE_LENGTH, SEQUENCE_COUNT, 2))
    return {"queries": queries, "keys_in": keys_in, "values_in": values_in, "log_decay": log_decay, "attn_gain": attn_gain, "out_weight": out_weight, "residual": residual, "moe_gain": moe_gain, "router": router, "gate_weight": gate_weight, "up_weight": up_weight, "down_weight": down_weight, "routes": routes}


highest = lax.Precision.HIGHEST

def silu_float(values):
    return values * jax.nn.sigmoid(values)

def lightning(queries, keys_in, values_in, log_decay):
    blocks = SEQUENCE_LENGTH // SPAN
    q_all = silu_float(queries.astype(jnp.float32)).reshape(blocks, SPAN, SEQUENCE_COUNT, HEAD_TOTAL, HD)
    k_all = silu_float(keys_in.astype(jnp.float32)).reshape(blocks, SPAN, SEQUENCE_COUNT, HEAD_TOTAL, HD)
    v_all = values_in.astype(jnp.float32).reshape(blocks, SPAN, SEQUENCE_COUNT, HEAD_TOTAL, HD)
    decay_blocks = jnp.transpose(log_decay.reshape(HEAD_TOTAL, SEQUENCE_COUNT, blocks, SPAN), (2, 1, 0, 3))
    positions = jnp.arange(SPAN, dtype=jnp.int32)
    causal = positions[:, None] >= positions[None, :]

    def advance(state, pieces):
        q_block, k_block, v_block, decay_block = pieces
        cumulative = jnp.cumsum(decay_block, axis=-1)
        spacing = cumulative[..., :, None] - cumulative[..., None, :]
        damping = jnp.where(causal, jnp.exp(jnp.where(causal, spacing, 0.0)), 0.0)
        scores = jnp.einsum('tshd,ushd->shtu', q_block, k_block, precision=highest) * damping
        inside = jnp.einsum('shtu,ushe->tshe', scores, v_block, precision=highest)
        carried = jnp.exp(jnp.transpose(cumulative, (2, 0, 1)))[..., None] * jnp.einsum('tshd,shde->tshe', q_block, state, precision=highest)
        remaining = jnp.exp(cumulative[..., -1:] - cumulative)
        fresh_state = jnp.einsum('ushd,ushe->shde', k_block * jnp.transpose(remaining, (2, 0, 1))[..., None], v_block, precision=highest)
        new_state = jnp.exp(cumulative[..., -1])[..., None, None] * state + fresh_state
        return (new_state, inside + carried)
    start_state = jnp.zeros((SEQUENCE_COUNT, HEAD_TOTAL, HD, HD), jnp.float32)
    _, outputs = lax.scan(advance, start_state, (q_all, k_all, v_all, decay_blocks))
    return outputs.reshape(SEQUENCE_LENGTH, SEQUENCE_COUNT, HEAD_TOTAL, HD)

def reference(queries, keys_in, values_in, log_decay, attn_gain, out_weight, residual, moe_gain, router, gate_weight, up_weight, down_weight, routes):
    tokens = SEQUENCE_LENGTH * SEQUENCE_COUNT
    heads_out = lightning(queries, keys_in, values_in, log_decay)
    mean_square = lax.optimization_barrier(jnp.mean(heads_out * heads_out, axis=-1, keepdims=True))
    normed_heads = (heads_out * lax.rsqrt(mean_square + 1e-06) * attn_gain.reshape(HEAD_TOTAL, HD)).astype(jnp.bfloat16)
    grouped = jnp.transpose(normed_heads.reshape(tokens, N_EP, HEADS_DEV * HD), (1, 0, 2))
    grouped_weight = out_weight.reshape(N_EP, HEADS_DEV * HD, D)

    def add_group(running, pieces):
        group_in, group_weight = pieces
        partial_value = jnp.dot(group_in, group_weight, preferred_element_type=jnp.float32).astype(jnp.bfloat16)
        partial_value = lax.optimization_barrier(partial_value).astype(jnp.float32)
        return (running + partial_value, None)
    attn, _ = lax.scan(add_group, jnp.zeros((tokens, D), jnp.float32), (grouped, grouped_weight))
    hidden_state = residual.reshape(tokens, D).astype(jnp.float32) + attn
    moe_scale = lax.rsqrt(lax.optimization_barrier(jnp.mean(hidden_state * hidden_state, axis=-1, keepdims=True)) + 1e-06)
    moe_in = (hidden_state * moe_scale * moe_gain).astype(jnp.bfloat16)
    logits = jnp.dot(moe_in, router, preferred_element_type=jnp.float32)
    expert_ids = routes.reshape(tokens, 2).astype(jnp.int32)
    picked = jnp.take_along_axis(logits, expert_ids, axis=1)
    weight_first = jax.nn.sigmoid(picked[:, 0] - picked[:, 1])
    weight_second = jax.nn.sigmoid(picked[:, 1] - picked[:, 0])
    blocks = tokens // ROWS
    block_ids = expert_ids.reshape(blocks, 2 * ROWS)
    route_hot = (block_ids[..., None] == jnp.arange(EXPERTS, dtype=jnp.int32)).astype(jnp.int32)
    earlier = jnp.cumsum(route_hot, axis=1) - route_hot
    slots = lax.optimization_barrier(jnp.sum(earlier * route_hot, axis=-1)).astype(jnp.int32)
    owner_row = jnp.repeat(jnp.arange(tokens, dtype=jnp.int32).reshape(blocks, ROWS), 2, axis=1)
    block_index = jnp.broadcast_to(jnp.arange(blocks, dtype=jnp.int32)[:, None], (blocks, 2 * ROWS))
    table = jnp.full((EXPERTS, blocks, CAP), tokens, jnp.int32)
    table = table.at[block_ids, block_index, slots].set(owner_row)
    padded_in = jnp.concatenate([moe_in, jnp.zeros((1, D), jnp.bfloat16)], axis=0)
    expert_inputs = padded_in[table.reshape(EXPERTS, blocks * CAP)]

    def one_expert(pieces):
        rows_in, gate_part, up_part, down_part = pieces
        gate_out = jnp.dot(rows_in, gate_part, preferred_element_type=jnp.float32)
        up_out = jnp.dot(rows_in, up_part, preferred_element_type=jnp.float32)
        expert_hidden = (silu_float(gate_out) * up_out).astype(jnp.bfloat16)
        hidden_groups = jnp.transpose(expert_hidden.reshape(blocks * CAP, N_CTX, FF // N_CTX), (1, 0, 2))
        down_groups = down_part.reshape(N_CTX, FF // N_CTX, D)

        def add_slice(running, sliced):
            slice_hidden, slice_down = sliced
            partial_value = jnp.dot(slice_hidden, slice_down, preferred_element_type=jnp.float32).astype(jnp.bfloat16)
            partial_value = lax.optimization_barrier(partial_value).astype(jnp.float32)
            return (running + partial_value, None)
        summed, _ = lax.scan(add_slice, jnp.zeros((blocks * CAP, D), jnp.float32), (hidden_groups, down_groups))
        return summed.astype(jnp.bfloat16)
    expert_out = lax.map(one_expert, (expert_inputs, gate_weight, up_weight, down_weight))
    flat_index = block_ids * (blocks * CAP) + block_index * CAP + slots
    fetched = expert_out.reshape(EXPERTS * blocks * CAP, D)[flat_index.reshape(tokens, 2)].astype(jnp.float32)
    mixed = hidden_state + weight_first[:, None] * fetched[:, 0] + weight_second[:, None] * fetched[:, 1]
    return mixed.astype(jnp.bfloat16).reshape(SEQUENCE_LENGTH, SEQUENCE_COUNT, D)
```

```python
import jax
import jax.numpy as jnp
import numpy as np
from jax import lax
from jax.experimental import pallas as pl
from jax.experimental.pallas import tpu as pltpu
from jax.sharding import PartitionSpec as P

MESH = pl.DeviceIdType.MESH
F32, BF16 = jnp.float32, jnp.bfloat16
CW = 1024


def place_of():
    ctx, ep = lax.axis_index("ctx"), lax.axis_index("ep")
    y, core = lax.rem(ctx, 8) // 2, lax.rem(ctx, 2)
    z = (ctx // 8) * 4 + lax.rem(ep, 4)
    return ep // 4, y, z, core


def device_at(x, y, z, core):
    return ((z // 4) * 8 + y * 2 + core, x * 4 + lax.rem(z, 4))


def mm(a, b):
    return jnp.dot(a, b, preferred_element_type=F32)


def rows(start, size):
    return pl.ds(pl.multiple_of(start, size), size)


def moe_kernel(
    nh_ref, wo_ref, res_ref, gain_ref, router_ref, place_ref, hot0_ref, hot1_ref, pick0_ref, pick1_ref,
    q_ref, qt_ref, pack_ref, unpack_ref, gate_hbm, up_hbm, down_hbm, gate_peer, up_peer, down_peer,
    out_ref,
    wg, wu, wd, part, c1_opp, c1_nb, c2_out, c2_in, hid, ssq, sent, d1_in, d2_out, d2_in, tok, logits,
    acc, act, f_opp, f_nb, g2_out, g2_in, g3_out, g3_in,
    load_sem,
    c1o_s, c1o_r, c1n_s, c1n_r, c2_s, c2_r, d1_s, d1_r, d2_s, d2_r, d3n_s, d3n_r, d3f_s, d3f_r,
    fo_s, fo_r, fn_s, fn_r, g2_s, g2_r, g3_s, g3_r,
):
    x, y, z, core = place_of()
    zl, zh = lax.rem(z, 4), z // 4
    chunks = hid.shape[0]

    def at_x(d):
        return device_at(lax.rem(x + d, 4), y, z, core)

    def at_y(d):
        return device_at(x, lax.rem(y + d, 4), z, core)

    def at_z(d):
        return device_at(x, y, lax.rem(z + d, 8), core)

    def at_line(d):
        return device_at(x, y, zh * 4 + lax.rem(zl + d, 4), core)

    def copy(src, dst, send, recv, to):
        return pltpu.make_async_remote_copy(
            src_ref=src, dst_ref=dst, send_sem=send, recv_sem=recv, device_id=to, device_id_type=MESH
        )

    barrier = pltpu.get_barrier_semaphore()
    peers = [at_x(d) for d in (1, 2, 3)] + [at_y(1), at_y(3)] + [at_z(d) for d in range(1, 8)]
    for peer in peers:
        pl.semaphore_signal(barrier, inc=1, device_id=peer, device_id_type=MESH)

    def loads(act_on):
        for i, (g, u, d) in enumerate(((gate_hbm, up_hbm, down_hbm), (gate_peer, up_peer, down_peer))):
            @pl.loop(0, chunks)
            def _(j):
                span = rows(j * CW, CW)
                act_on(pltpu.make_async_copy(g.at[0, span, :], wg.at[i, j], load_sem.at[i, 0, j]))
                act_on(pltpu.make_async_copy(u.at[0, span, :], wu.at[i, j], load_sem.at[i, 1, j]))
                act_on(pltpu.make_async_copy(d.at[0, :, span], wd.at[i, j], load_sem.at[i, 2, j]))

    loads(lambda c: c.start())
    ssq[...] = jnp.zeros_like(ssq)
    logits[...] = jnp.zeros_like(logits)
    acc[...] = jnp.zeros_like(acc)
    pl.semaphore_wait(barrier, len(peers))

    def ring_copies(j, buf, size, opp, near, so, ro, sn, rn, at, mine):
        half = size // 2
        far = rows(lax.rem(mine + 2, 4) * size, size)
        far_a = pl.ds(pl.multiple_of(lax.rem(mine + 2, 4) * size, size), half)
        far_b = pl.ds(pl.multiple_of(lax.rem(mine + 2, 4) * size + half, half), half)
        del far
        right = rows(lax.rem(mine + 1, 4) * size, size)
        left = rows(lax.rem(mine + 3, 4) * size, size)
        return (
            copy(buf.at[j, far_a], opp.at[j, 0], so.at[j, 0], ro.at[j, 0], at(1)),
            copy(buf.at[j, far_b], opp.at[j, 1], so.at[j, 1], ro.at[j, 1], at(3)),
            copy(buf.at[j, right], near.at[j, 0], sn.at[j, 0], rn.at[j, 0], at(1)),
            copy(buf.at[j, left], near.at[j, 1], sn.at[j, 1], rn.at[j, 1], at(3)),
        )

    def ring_forward(j, buf, size, opp, copies, mine):
        half = size // 2
        copies[0].wait_recv()
        to_right = pl.ds(pl.multiple_of(lax.rem(mine + 1, 4) * size, size), half)
        buf[j, to_right] = (buf[j, to_right].astype(F32) + opp[j, 0].astype(F32)).astype(BF16)
        copies[2].start()
        copies[1].wait_recv()
        to_left = pl.ds(pl.multiple_of(lax.rem(mine + 3, 4) * size + half, half), half)
        buf[j, to_left] = (buf[j, to_left].astype(F32) + opp[j, 1].astype(F32)).astype(BF16)
        copies[3].start()

    def ring_total(j, buf, size, near, copies, mine):
        copies[2].wait_recv()
        copies[3].wait_recv()
        own = rows(mine * size, size)
        return buf[j, own].astype(F32) + near[j, 0].astype(F32) + near[j, 1].astype(F32)

    def c1(j):
        return ring_copies(j, part, 64, c1_opp, c1_nb, c1o_s, c1o_r, c1n_s, c1n_r, at_x, x)

    def c2(j, d):
        to = rows(lax.rem(zl + d, 4) * 16, 16)
        return copy(c2_out.at[j, to], c2_in.at[j, d - 1], c2_s.at[j, d - 1], c2_r.at[j, d - 1], at_line(d))

    def c_step(s, _):
        @pl.when(s < chunks)
        def _():
            j = s
            part[j] = mm(nh_ref[...], wo_ref[:, rows(j * CW, CW)]).astype(BF16)
            copies = c1(j)
            copies[0].start()
            copies[1].start()

        @pl.when((s >= 1) & (s < chunks + 1))
        def _():
            j = s - 1
            ring_forward(j, part, 64, c1_opp, c1(j), x)

        @pl.when((s >= 2) & (s < chunks + 2))
        def _():
            j = s - 2
            c2_out[j] = ring_total(j, part, 64, c1_nb, c1(j), x).astype(BF16)
            for d in (3, 2, 1):
                c2(j, d).start()

        @pl.when(s >= 3)
        def _():
            j = s - 3
            span = rows(j * CW, CW)
            total = c2_out[j, rows(zl * 16, 16)].astype(F32)
            for d in (1, 2, 3):
                c2(j, d).wait_recv()
                total = total + c2_in[j, d - 1].astype(F32)
            state = res_ref[:, span].astype(F32) + total
            hid[j] = state
            ssq[...] += jnp.sum(state * state, axis=-1, keepdims=True)

        return 0

    lax.fori_loop(0, chunks + 3, c_step, 0)
    scale = lax.rsqrt(ssq[:, 0:1] * (1.0 / (chunks * CW)) + 1e-06)

    def d1(j, d):
        to = rows(lax.rem(x + d, 4) * 16, 16)
        return copy(sent.at[j, to], d1_in.at[j, rows(x * 16, 16)], d1_s.at[j, d - 1], d1_r.at[j, d - 1], at_x(d))

    def d1_wait(j, d):
        source = rows(lax.rem(x + 4 - d, 4) * 16, 16)
        copy(sent.at[j, source], d1_in.at[j, source], d1_s.at[j, d - 1], d1_r.at[j, d - 1], at_x(d)).wait_recv()

    def d2(j, d):
        to = rows(lax.rem(zl + d, 4) * 16, 16)
        return copy(d2_out.at[j, to], d2_in.at[j, rows(z * 16, 16)], d2_s.at[j, d - 1], d2_r.at[j, d - 1], at_z(d))

    def d2_wait(j, d):
        source = rows(lax.rem(z + 8 - d, 8) * 16, 16)
        copy(
            d2_out.at[j, pl.ds(0, 16)], d2_in.at[j, source], d2_s.at[j, d - 1], d2_r.at[j, d - 1], at_z(d)
        ).wait_recv()

    def block(d):
        return rows(lax.rem(y + d, 4) * 96, 96)

    def d3_near(j, side):
        own = block(0)
        return copy(tok.at[j, own], tok.at[j, own], d3n_s.at[j, side], d3n_r.at[j, side], at_y(3 if side else 1))

    def d3_near_wait(j, side):
        source = block(1 if side else 3)
        copy(tok.at[j, source], tok.at[j, source], d3n_s.at[j, side], d3n_r.at[j, side], at_y(1)).wait_recv()

    def half_of(d, side):
        return pl.ds(pl.multiple_of(lax.rem(y + d, 4) * 96 + 48 * side, 48), 48)

    def d3_far(j, side):
        span = half_of(1 if side else 3, side)
        return copy(tok.at[j, span], tok.at[j, span], d3f_s.at[j, side], d3f_r.at[j, side], at_y(3 if side else 1))

    def d3_far_wait(j, side):
        span = half_of(2, side)
        copy(tok.at[j, span], tok.at[j, span], d3f_s.at[j, side], d3f_r.at[j, side], at_y(1)).wait_recv()

    def d_step(s, _):
        @pl.when(s < chunks)
        def _():
            j = s
            span = rows(j * CW, CW)
            moe_in = (hid[j] * scale * gain_ref[:, span]).astype(BF16)
            sent[j] = mm(place_ref[...], moe_in).astype(BF16)
            for d in (2, 1, 3):
                d1(j, d).start()
            d1_in[j, rows(x * 16, 16)] = sent[j, rows(x * 16, 16)]
            logits[...] += mm(moe_in, router_ref[span, :])

        @pl.when((s >= 1) & (s < chunks + 1))
        def _():
            j = s - 1
            for d in (1, 2, 3):
                d1_wait(j, d)
            d2_out[j] = mm(q_ref[...], d1_in[j]).astype(BF16)
            for d in (4, 3, 5, 2, 6, 1, 7):
                d2(j, d).start()
            d2_in[j, rows(z * 16, 16)] = d2_out[j, rows(zl * 16, 16)]

        @pl.when((s >= 2) & (s < chunks + 2))
        def _():
            j = s - 2
            for d in range(1, 8):
                d2_wait(j, d)
            tok[j, block(0)] = mm(pack_ref[...], d2_in[j]).astype(BF16)
            d3_near(j, 0).start()
            d3_near(j, 1).start()

        @pl.when((s >= 3) & (s < chunks + 3))
        def _():
            j = s - 3
            for side in (0, 1):
                d3_near_wait(j, side)
                d3_far(j, side).start()

        @pl.when(s >= 4)
        def _():
            j = s - 4
            for side in (0, 1):
                d3_far_wait(j, side)
            tokens = tok[j]
            for i in range(2):
                acc[i, 0] += mm(tokens, wg[i, j])
                acc[i, 1] += mm(tokens, wu[i, j])

        return 0

    loads(lambda c: c.wait())
    lax.fori_loop(0, chunks + 4, d_step, 0)
    for i in range(2):
        gate = acc[i, 0]
        act[i] = (gate * jax.nn.sigmoid(gate) * acc[i, 1]).astype(BF16)

    @pl.loop(0, chunks)
    def _(j):
        for side in (0, 1):
            d3_near(j, side).wait_send()
            d3_far(j, side).wait_send()

    picked0 = jnp.sum(logits[...] * pick0_ref[...], axis=-1, keepdims=True)
    picked1 = jnp.sum(logits[...] * pick1_ref[...], axis=-1, keepdims=True)
    mix = jax.nn.sigmoid(picked0 - picked1) * hot0_ref[...] + jax.nn.sigmoid(picked1 - picked0) * hot1_ref[...]
    mix_hi = mix.astype(BF16)
    mix_lo = (mix - mix_hi.astype(F32)).astype(BF16)

    def f1(j):
        return ring_copies(j, tok, 96, f_opp, f_nb, fo_s, fo_r, fn_s, fn_r, at_y, y)

    def g2(j, d):
        to = rows(lax.rem(z + d, 8) * 16, 16)
        return copy(g2_out.at[j, to], g2_in.at[j, rows(z * 16, 16)], g2_s.at[j, d - 1], g2_r.at[j, d - 1], at_z(d))

    def g2_wait(j, d):
        source = rows(lax.rem(z + 8 - d, 8) * 16, 16)
        copy(
            g2_out.at[j, source], g2_in.at[j, source], g2_s.at[j, d - 1], g2_r.at[j, d - 1], at_z(d)
        ).wait_recv()

    def g3(j, d):
        to = rows(lax.rem(x + d, 4) * 16, 16)
        return copy(g3_out.at[j, to], g3_in.at[j, rows(x * 16, 16)], g3_s.at[j, d - 1], g3_r.at[j, d - 1], at_x(d))

    def g3_wait(j, d):
        source = rows(lax.rem(x + 4 - d, 4) * 16, 16)
        copy(
            g3_out.at[j, source], g3_in.at[j, source], g3_s.at[j, d - 1], g3_r.at[j, d - 1], at_x(d)
        ).wait_recv()

    def f_step(s, _):
        @pl.when(s < chunks)
        def _():
            j = s
            tok[j] = (mm(act[0], wd[0, j]) + mm(act[1], wd[1, j])).astype(BF16)
            copies = f1(j)
            copies[0].start()
            copies[1].start()

        @pl.when((s >= 1) & (s < chunks + 1))
        def _():
            j = s - 1
            ring_forward(j, tok, 96, f_opp, f1(j), y)

        @pl.when((s >= 2) & (s < chunks + 2))
        def _():
            j = s - 2
            total = ring_total(j, tok, 96, f_nb, f1(j), y).astype(BF16)
            g2_out[j] = mm(unpack_ref[...], total).astype(BF16)
            for d in (4, 3, 5, 2, 6, 1, 7):
                g2(j, d).start()
            g2_in[j, rows(z * 16, 16)] = g2_out[j, rows(z * 16, 16)]

        @pl.when((s >= 3) & (s < chunks + 3))
        def _():
            j = s - 3
            for d in range(1, 8):
                g2_wait(j, d)
            total = (g2_in[j, pl.ds(0, 64)].astype(F32) + g2_in[j, pl.ds(64, 64)].astype(F32)).astype(BF16)
            g3_out[j] = mm(qt_ref[...], total).astype(BF16)
            for d in (2, 1, 3):
                g3(j, d).start()
            g3_in[j, rows(x * 16, 16)] = g3_out[j, rows(x * 16, 16)]

        @pl.when(s >= 4)
        def _():
            j = s - 4
            for d in (1, 2, 3):
                g3_wait(j, d)
            back = g3_in[j]
            out_ref[:, rows(j * CW, CW)] = (hid[j] + mm(mix_hi, back) + mm(mix_lo, back)).astype(BF16)

        return 0

    lax.fori_loop(0, chunks + 4, f_step, 0)

    @pl.loop(0, chunks)
    def _(j):
        for c in c1(j) + f1(j):
            c.wait_send()
        for d in (1, 2, 3):
            c2(j, d).wait_send()
            d1(j, d).wait_send()
            g3(j, d).wait_send()
        for d in range(1, 8):
            d2(j, d).wait_send()
            g2(j, d).wait_send()


def selections():
    q = np.zeros((64, 64), np.float32)
    pack = np.zeros((96, 128), np.float32)
    for e in range(4):
        for source in range(4):
            for s in range(3):
                q[e * 16 + source * 3 + s, source * 16 + e * 4 + s] = 1
    for source in range(8):
        for r in range(12):
            pack[source * 12 + r, source * 16 + r] = 1
    return tuple(jnp.asarray(a, BF16) for a in (q, q.T, pack, pack.T))


def moe_block(nh, wo, residual, moe_gain, router, routes, experts, peer_experts):
    count, width = residual.shape
    chunks = width // CW
    hidden = experts[0].shape[2]
    number = router.shape[1]
    ids = routes.reshape(count, 2)
    hot = ids[..., None] == jnp.arange(number, dtype=jnp.int32)
    flat = hot.reshape(2 * count, number).astype(jnp.int32)
    slots = jnp.sum((jnp.cumsum(flat, axis=0) - flat) * flat, axis=-1).reshape(count, 2)
    target = ids * 4 + slots
    hots = (target[..., None] == jnp.arange(number * 4, dtype=jnp.int32)).astype(F32)
    picks = hot.astype(F32)
    place = (hots[:, 0] + hots[:, 1]).astype(BF16).T
    n = chunks
    dma = lambda *shape: pltpu.SemaphoreType.DMA(shape)
    vmem = lambda *shape: pltpu.VMEM(shape, BF16)
    scratch = [
        vmem(2, n, CW, hidden), vmem(2, n, CW, hidden), vmem(2, n, hidden, CW),
        vmem(n, 256, CW), vmem(n, 2, 32, CW), vmem(n, 2, 64, CW), vmem(n, 64, CW), vmem(n, 3, 16, CW),
        pltpu.VMEM((n, 16, CW), F32), pltpu.VMEM((16, 128), F32),
        vmem(n, 64, CW), vmem(n, 64, CW), vmem(n, 64, CW), vmem(n, 128, CW), vmem(n, 384, CW),
        pltpu.VMEM((16, 16), F32), pltpu.VMEM((2, 2, 384, hidden), F32), vmem(2, 384, hidden),
        vmem(n, 2, 48, CW), vmem(n, 2, 96, CW), vmem(n, 128, CW), vmem(n, 128, CW), vmem(n, 64, CW), vmem(n, 64, CW),
        dma(2, 3, n),
    ]
    for lanes in (2, 2, 3, 3, 7, 2, 2, 2, 2, 7, 3):
        scratch += [dma(n, lanes), dma(n, lanes)]
    in_vmem = pl.BlockSpec(memory_space=pltpu.VMEM)
    in_hbm = pl.BlockSpec(memory_space=pl.ANY)
    return pl.pallas_call(
        moe_kernel,
        out_shape=jax.ShapeDtypeStruct((count, width), BF16),
        in_specs=[in_vmem] * 14 + [in_hbm] * 6,
        out_specs=in_vmem,
        scratch_shapes=scratch,
        compiler_params=pltpu.CompilerParams(
            collective_id=0, has_side_effects=True, vmem_limit_bytes=67043328
        ),
    )(
        nh, wo, residual, moe_gain.reshape(1, width), router, place, hots[:, 0], hots[:, 1], picks[:, 0], picks[:, 1],
        *selections(), *experts, *peer_experts,
    )


highest = lax.Precision.HIGHEST


def entering(array, axis, join, neutral):
    place = lax.axis_index(axis)
    gathered = jax.tree.map(
        lambda a, kind: lax.all_gather(a.astype(kind), axis), array, (jnp.bfloat16, jnp.bfloat16)
    )
    state = jax.tree.map(lambda a, e: jnp.zeros_like(a) + jnp.asarray(e, a.dtype), array, neutral)

    def one(hop, state):
        return join(
            state,
            jax.tree.map(
                lambda a, own: lax.dynamic_index_in_dim(a, hop, 0, False).astype(own.dtype),
                gathered,
                array,
            ),
        )

    return lax.fori_loop(0, place, one, state)


def silu_float(values):
    return values * jax.nn.sigmoid(values)


def shards(
    queries,
    keys_in,
    values_in,
    log_decay,
    attn_gain,
    out_weight,
    residual,
    moe_gain,
    router,
    gate_weight,
    up_weight,
    down_weight,
    routes,
):
    length, sequences, width = queries.shape
    head_count = log_decay.shape[0]
    head_size = width // head_count
    q_local = silu_float(queries.astype(jnp.float32)).reshape(
        length, sequences, head_count, head_size
    )
    k_local = silu_float(keys_in.astype(jnp.float32)).reshape(
        length, sequences, head_count, head_size
    )
    v_local = values_in.astype(jnp.float32).reshape(length, sequences, head_count, head_size)
    cumulative = jnp.cumsum(jnp.transpose(log_decay, (1, 0, 2)), axis=-1)
    positions = jnp.arange(length, dtype=jnp.int32)
    causal = positions[:, None] >= positions[None, :]
    spacing = cumulative[..., :, None] - cumulative[..., None, :]
    damping = jnp.where(causal, jnp.exp(jnp.where(causal, spacing, 0.0)), 0.0)
    scores = jnp.einsum("tshd,ushd->shtu", q_local, k_local, precision=highest) * damping
    inside = jnp.einsum("shtu,ushe->tshe", scores, v_local, precision=highest)
    remaining = jnp.exp(cumulative[..., -1:] - cumulative)
    own_state = jnp.einsum(
        "ushd,ushe->shde",
        k_local * jnp.transpose(remaining, (2, 0, 1))[..., None],
        v_local,
        precision=highest,
    )
    block_log = cumulative[..., -1]

    def combine(earlier, later_part):
        return (
            earlier[0] * later_part[0],
            later_part[0][..., None, None] * earlier[1] + later_part[1],
        )

    identity = (jnp.ones_like(block_log), jnp.zeros_like(own_state))
    _, prefix_state = entering((jnp.exp(block_log), own_state), "ctx", combine, identity)
    carried = jnp.exp(jnp.transpose(cumulative, (2, 0, 1)))[..., None] * jnp.einsum(
        "tshd,shde->tshe", q_local, prefix_state, precision=highest
    )
    heads_out = inside + carried
    mean_square = jnp.mean(heads_out * heads_out, axis=-1, keepdims=True)
    normed_heads = (
        heads_out * lax.rsqrt(mean_square + 1e-06) * attn_gain.reshape(head_count, head_size)
    )
    normed_heads = normed_heads.astype(jnp.bfloat16).reshape(length * sequences, width)
    experts = (gate_weight, up_weight, down_weight)
    swap = [(i, i ^ 1) for i in range(lax.axis_size("ctx"))]
    peer_experts = tuple(lax.ppermute(w, "ctx", swap) for w in experts)
    mixed = moe_block(
        normed_heads,
        lax.all_gather(out_weight, "ctx", axis=1, tiled=True),
        residual.reshape(residual.shape[0], -1),
        moe_gain,
        router,
        routes,
        experts,
        peer_experts,
    )
    return mixed.reshape(residual.shape)


def solution(mesh):
    return jax.shard_map(
        shards,
        mesh=mesh,
        in_specs=(
            P("ctx", None, "ep"),
            P("ctx", None, "ep"),
            P("ctx", None, "ep"),
            P("ep", None, "ctx"),
            P("ep"),
            P("ep", "ctx"),
            P(("ctx", "ep"), None, None),
            P(),
            P(),
            P("ep", None, "ctx"),
            P("ep", None, "ctx"),
            P("ep", "ctx", None),
            P(("ctx", "ep"), None, None),
        ),
        out_specs=P(("ctx", "ep"), None, None),
        check_vma=False,
    )
```

```python
import jax
import jax.numpy as jnp
import numpy as np
from jax import lax
from jax.experimental import pallas as pl
from jax.experimental.pallas import tpu as pltpu
from jax.sharding import PartitionSpec as P

MESH = pl.DeviceIdType.MESH
F32, BF16 = jnp.float32, jnp.bfloat16
CW = 768
HEAD = 128


def silu_float(values):
    return values * jax.nn.sigmoid(values)


def place_of():
    ctx, ep = lax.axis_index("ctx"), lax.axis_index("ep")
    y, core = lax.rem(ctx, 8) // 2, lax.rem(ctx, 2)
    z = (ctx // 8) * 4 + lax.rem(ep, 4)
    return ep // 4, y, z, core


def device_at(x, y, z, core):
    return ((z // 4) * 8 + y * 2 + core, x * 4 + lax.rem(z, 4))


def mm(a, b):
    return jnp.dot(a, b, preferred_element_type=F32)


def mm_nt(a, b, precision=None):
    return lax.dot_general(a, b, (((1,), (1,)), ((), ())), precision=precision, preferred_element_type=F32)


def mm_tn(a, b, precision=None):
    return lax.dot_general(a, b, (((0,), (0,)), ((), ())), precision=precision, preferred_element_type=F32)


def rows(start, size):
    return pl.ds(pl.multiple_of(start, size), size)


def block_kernel(
    queries, keys, values, decay_ref, head_gain, ow_hbm, res_ref, gain_ref, router_ref, routes_ref,
    q_ref, qt_ref, pack_ref, unpack_ref, gate_hbm, up_hbm, down_hbm,
    out_ref,
    nh, wo, inside, s1_out, s1_in, s2, s3_out, s3_in,
    wg, wu, wd, part, c1_opp, c1_nb, c2_out, c2_in, hid, ssq, sent, d1_in, d2_out, d2_in, tok, logits,
    acc, act, f_opp, f_nb, g2_out, g2_in, g3_out, g3_in,
    load_sem, swap_s, swap_r, s1_s, s1_r, s2_s, s2_r, s3_s, s3_r,
    bc_s, bc_r, bz_s, bz_r, bn_s, bn_r, bf_s, bf_r,
    c1o_s, c1o_r, c1n_s, c1n_r, c2_s, c2_r, d1_s, d1_r, d2_s, d2_r, d3n_s, d3n_r, d3f_s, d3f_r,
    fo_s, fo_r, fn_s, fn_r, g2_s, g2_r, g3_s, g3_r,
):
    x, y, z, core = place_of()
    zl, zh = lax.rem(z, 4), z // 4
    chunks = hid.shape[0]

    def at_x(d):
        return device_at(lax.rem(x + d, 4), y, z, core)

    def at_y(d):
        return device_at(x, lax.rem(y + d, 4), z, core)

    def at_z(d):
        return device_at(x, y, lax.rem(z + d, 8), core)

    def at_line(d):
        return device_at(x, y, zh * 4 + lax.rem(zl + d, 4), core)

    def copy(src, dst, send, recv, to):
        return pltpu.make_async_remote_copy(
            src_ref=src, dst_ref=dst, send_sem=send, recv_sem=recv, device_id=to, device_id_type=MESH
        )

    twin = device_at(x, y, z, 1 - core)
    barrier = pltpu.get_barrier_semaphore()
    peers = [twin] + [at_x(d) for d in (1, 2, 3)] + [at_y(d) for d in (1, 2, 3)] + [at_z(d) for d in range(1, 8)]
    for peer in peers:
        pl.semaphore_signal(barrier, inc=1, device_id=peer, device_id_type=MESH)
    weights = ((gate_hbm.at[0], wg), (up_hbm.at[0], wu), (down_hbm.at[0], wd))
    own_loads = [pltpu.make_async_copy(w, to.at[0], load_sem.at[i]) for i, (w, to) in enumerate(weights)]
    swaps = [copy(w, to.at[1], swap_s.at[i], swap_r.at[i], twin) for i, (w, to) in enumerate(weights)]
    ssq[...] = jnp.zeros_like(ssq)
    logits[...] = jnp.zeros_like(logits)
    acc[...] = jnp.zeros_like(acc)

    length = queries.shape[0]
    at_t = lax.broadcasted_iota(jnp.int32, (length, length), 0)
    at_u = lax.broadcasted_iota(jnp.int32, (length, length), 1)
    highest = lax.Precision.HIGHEST
    own_state, own_decay, cumulative = [], [], []
    for h in range(2):
        lanes = pl.ds(h * HEAD, HEAD)
        log_row = decay_ref[h : h + 1, :]
        log_col = jnp.sum(jnp.where(at_u == at_t, log_row, 0.0), axis=1, keepdims=True)
        cum_col = jnp.sum(jnp.where(at_u <= at_t, log_row, 0.0), axis=1, keepdims=True)
        cum_row = jnp.sum(jnp.where(at_t <= at_u, log_col, 0.0), axis=0, keepdims=True)
        last = jnp.sum(log_row, axis=1, keepdims=True)
        k = silu_float(keys[:, lanes].astype(F32))
        own_state.append(mm_tn(k * jnp.exp(last - cum_col), values[:, lanes].astype(F32), highest))
        own_decay.append(jnp.broadcast_to(jnp.exp(last), (1, HEAD)))
        cumulative.append((cum_col, cum_row))

    def write_state(to, h, state, decay):
        high = decay.astype(BF16)
        low = (decay - high.astype(F32)).astype(BF16)
        first = lax.broadcasted_iota(jnp.int32, (16, HEAD), 0) == 0
        to[h, pl.ds(0, HEAD)] = state.astype(BF16)
        to[h, pl.ds(HEAD, 16)] = jnp.where(first, high.astype(F32), low.astype(F32)).astype(BF16)

    def read_state(of, h):
        tail = of[h, pl.ds(HEAD, 16)].astype(F32)
        return of[h, pl.ds(0, HEAD)].astype(F32), tail[0:1, :] + tail[1:2, :]

    for h in range(2):
        write_state(s1_out, h, own_state[h], own_decay[h])
    pl.semaphore_wait(barrier, len(peers))
    state1 = copy(s1_out, s1_in, s1_s, s1_r, twin)
    state1.start()

    mine = pl.ds(pl.multiple_of(core * 384, 128), 384)
    others = pl.ds(pl.multiple_of((1 - core) * 384, 128), 384)

    def chip_of(group, d):
        return lax.rem(zh + group, 2) * 4 + lax.rem(y + d, 4)

    def b_core(group, d):
        src = wo.at[chip_of(group, d), :, mine]
        return copy(ow_hbm if (group, d) == (0, 0) else src, src, bc_s.at[group, d], bc_r.at[group, d], twin)

    def b_core_wait(group, d):
        to = wo.at[chip_of(group, d), :, others]
        copy(to, to, bc_s.at[group, d], bc_r.at[group, d], twin).wait_recv()

    def b_z():
        return copy(ow_hbm, wo.at[chip_of(0, 0), :, mine], bz_s, bz_r, at_z(4))

    def b_z_wait():
        to = wo.at[chip_of(1, 0), :, mine]
        copy(to, to, bz_s, bz_r, at_z(4)).wait_recv()

    def b_near(group, side):
        src = wo.at[chip_of(group, 0), :, mine]
        return copy(
            ow_hbm if group == 0 else src, src, bn_s.at[group, side], bn_r.at[group, side], at_y(3 if side else 1)
        )

    def b_near_wait(group, side):
        to = wo.at[chip_of(group, 1 if side else 3), :, mine]
        copy(to, to, bn_s.at[group, side], bn_r.at[group, side], at_y(1)).wait_recv()

    def b_far(group, side):
        to = wo.at[chip_of(group, 1 if side else 3), pl.ds(128 * side, 128), mine]
        return copy(to, to, bf_s.at[group, side], bf_r.at[group, side], at_y(3 if side else 1))

    def b_far_wait(group, side):
        to = wo.at[chip_of(group, 2), pl.ds(128 * side, 128), mine]
        copy(to, to, bf_s.at[group, side], bf_r.at[group, side], at_y(1)).wait_recv()

    def b_first(group):
        for side in (0, 1):
            b_near_wait(group, side)
            b_far(group, side).start()
            b_core(group, 1 if side else 3).start()

    def b_second(group):
        b_far_wait(group, 0)
        b_far_wait(group, 1)
        b_core(group, 2).start()

    own_columns = pltpu.make_async_copy(ow_hbm, wo.at[chip_of(0, 0), :, mine], load_sem.at[3])
    own_columns.start()
    b_z().start()
    b_near(0, 0).start()
    b_near(0, 1).start()
    b_core(0, 0).start()
    for c in swaps + own_loads:
        c.start()

    for h in range(2):
        lanes = pl.ds(h * HEAD, HEAD)
        cum_col, cum_row = cumulative[h]
        q = silu_float(queries[:, lanes].astype(F32))
        k = silu_float(keys[:, lanes].astype(F32))
        causal = at_t >= at_u
        damping = jnp.where(causal, jnp.exp(jnp.where(causal, cum_col - cum_row, 0.0)), 0.0)
        scores = mm_nt(q, k, highest) * damping
        inside[h] = jnp.dot(scores, values[:, lanes].astype(F32), precision=highest, preferred_element_type=F32)

    state1.wait_recv()
    first_core = core == 0
    twin_state = []
    for h in range(2):
        state, decay = read_state(s1_in, h)
        twin_state.append((state, decay))
        chip_state = jnp.where(
            first_core, decay * own_state[h] + state, own_decay[h] * state + own_state[h]
        )
        write_state(s2.at[y], h, chip_state, own_decay[h] * decay)

    def state2(d):
        return copy(s2.at[y], s2.at[y], s2_s.at[d - 1], s2_r.at[d - 1], at_y(d))

    for d in (2, 1, 3):
        state2(d).start()
    b_first(0)
    b_z_wait()
    b_near(1, 0).start()
    b_near(1, 1).start()
    b_core(1, 0).start()
    for d in (1, 2, 3):
        source = s2.at[lax.rem(y + 4 - d, 4)]
        copy(source, source, s2_s.at[d - 1], s2_r.at[d - 1], at_y(d)).wait_recv()
    entering = []
    for h in range(2):
        total = jnp.zeros((HEAD, HEAD), F32)
        before = jnp.zeros((HEAD, HEAD), F32)
        factor = jnp.ones((1, HEAD), F32)
        for other in range(4):
            state, decay = read_state(s2.at[other], h)
            before = jnp.where(other == y, total, before)
            factor = jnp.where(other < y, factor * decay, factor)
            total = decay * total + state
        s3_out[h] = total.astype(BF16)
        entering.append((before, factor))
    state3 = copy(s3_out, s3_in, s3_s, s3_r, at_z(4))

    @pl.when(zh == 0)
    def _():
        state3.start()
        s3_in[...] = jnp.zeros_like(s3_in)

    b_second(0)
    b_first(1)

    @pl.when(zh == 1)
    def _():
        state3.wait_recv()

    for h in range(2):
        lanes = pl.ds(h * HEAD, HEAD)
        before, factor = entering[h]
        state, decay = twin_state[h]
        prefix = factor * s3_in[h].astype(F32) + before
        prefix = jnp.where(first_core, prefix, decay * prefix + state)
        q = silu_float(queries[:, lanes].astype(F32))
        carried = jnp.dot(q, prefix, precision=highest, preferred_element_type=F32)
        heads_out = inside[h] + jnp.exp(cumulative[h][0]) * carried
        mean_square = jnp.mean(heads_out * heads_out, axis=-1, keepdims=True)
        nh[:, lanes] = (heads_out * lax.rsqrt(mean_square + 1e-06) * head_gain[:, lanes]).astype(BF16)
    b_second(1)
    own_columns.wait()
    for group in range(2):
        for d in range(4):
            b_core_wait(group, d)

    count, number = routes_ref.shape[0], router_ref.shape[0]
    expert = lax.broadcasted_iota(jnp.int32, (count, number), 1)
    picks = [(routes_ref[:, r : r + 1] == expert).astype(F32) for r in (0, 1)]
    earlier = lax.broadcasted_iota(jnp.int32, (count, count), 0) > lax.broadcasted_iota(jnp.int32, (count, count), 1)
    taken = mm(earlier.astype(F32).astype(BF16), (picks[0] + picks[1]).astype(BF16))
    slot = lax.broadcasted_iota(jnp.int32, (count, 4 * number), 1)
    hots = []
    for r in (0, 1):
        used = jnp.sum(taken * picks[r], axis=-1, keepdims=True).astype(jnp.int32)
        hots.append((routes_ref[:, r : r + 1] * 4 + used == slot).astype(F32))
    place = (hots[0] + hots[1]).astype(BF16)

    def ring_copies(j, buf, size, opp, near, so, ro, sn, rn, at, mine):
        half = size // 2
        far_a = pl.ds(pl.multiple_of(lax.rem(mine + 2, 4) * size, size), half)
        far_b = pl.ds(pl.multiple_of(lax.rem(mine + 2, 4) * size + half, half), half)
        right = rows(lax.rem(mine + 1, 4) * size, size)
        left = rows(lax.rem(mine + 3, 4) * size, size)
        return (
            copy(buf.at[j, far_a], opp.at[j, 0], so.at[j, 0], ro.at[j, 0], at(1)),
            copy(buf.at[j, far_b], opp.at[j, 1], so.at[j, 1], ro.at[j, 1], at(3)),
            copy(buf.at[j, right], near.at[j, 0], sn.at[j, 0], rn.at[j, 0], at(1)),
            copy(buf.at[j, left], near.at[j, 1], sn.at[j, 1], rn.at[j, 1], at(3)),
        )

    def ring_forward(j, buf, size, opp, copies, mine):
        half = size // 2
        copies[0].wait_recv()
        to_right = pl.ds(pl.multiple_of(lax.rem(mine + 1, 4) * size, size), half)
        buf[j, to_right] = (buf[j, to_right].astype(F32) + opp[j, 0].astype(F32)).astype(BF16)
        copies[2].start()
        copies[1].wait_recv()
        to_left = pl.ds(pl.multiple_of(lax.rem(mine + 3, 4) * size + half, half), half)
        buf[j, to_left] = (buf[j, to_left].astype(F32) + opp[j, 1].astype(F32)).astype(BF16)
        copies[3].start()

    def ring_total(j, buf, size, near, copies, mine):
        copies[2].wait_recv()
        copies[3].wait_recv()
        own = rows(mine * size, size)
        return buf[j, own].astype(F32) + near[j, 0].astype(F32) + near[j, 1].astype(F32)

    def c1(j):
        return ring_copies(j, part, 64, c1_opp, c1_nb, c1o_s, c1o_r, c1n_s, c1n_r, at_x, x)

    def c2(j, d):
        to = rows(lax.rem(zl + d, 4) * 16, 16)
        return copy(c2_out.at[j, to], c2_in.at[j, d - 1], c2_s.at[j, d - 1], c2_r.at[j, d - 1], at_line(d))

    def c_step(s, _):
        @pl.when(s < chunks)
        def _():
            j = s
            part[j] = mm(nh[...], wo[j]).astype(BF16)
            copies = c1(j)
            copies[0].start()
            copies[1].start()

        @pl.when((s >= 1) & (s < chunks + 1))
        def _():
            j = s - 1
            ring_forward(j, part, 64, c1_opp, c1(j), x)

        @pl.when((s >= 2) & (s < chunks + 2))
        def _():
            j = s - 2
            c2_out[j] = ring_total(j, part, 64, c1_nb, c1(j), x).astype(BF16)
            for d in (3, 2, 1):
                c2(j, d).start()

        @pl.when(s >= 3)
        def _():
            j = s - 3
            span = rows(j * CW, CW)
            total = c2_out[j, rows(zl * 16, 16)].astype(F32)
            for d in (1, 2, 3):
                c2(j, d).wait_recv()
                total = total + c2_in[j, d - 1].astype(F32)
            state = res_ref[:, span].astype(F32) + total
            hid[j] = state
            ssq[...] += jnp.sum(state * state, axis=-1, keepdims=True)

        return 0

    lax.fori_loop(0, chunks + 3, c_step, 0)
    scale = lax.rsqrt(ssq[:, 0:1] * (1.0 / (chunks * CW)) + 1e-06)

    def d1(j, d):
        to = rows(lax.rem(x + d, 4) * 16, 16)
        return copy(sent.at[j, to], d1_in.at[j, rows(x * 16, 16)], d1_s.at[j, d - 1], d1_r.at[j, d - 1], at_x(d))

    def d1_wait(j, d):
        source = rows(lax.rem(x + 4 - d, 4) * 16, 16)
        copy(sent.at[j, source], d1_in.at[j, source], d1_s.at[j, d - 1], d1_r.at[j, d - 1], at_x(d)).wait_recv()

    def d2(j, d):
        to = rows(lax.rem(zl + d, 4) * 16, 16)
        return copy(d2_out.at[j, to], d2_in.at[j, rows(z * 16, 16)], d2_s.at[j, d - 1], d2_r.at[j, d - 1], at_z(d))

    def d2_wait(j, d):
        source = rows(lax.rem(z + 8 - d, 8) * 16, 16)
        copy(
            d2_out.at[j, pl.ds(0, 16)], d2_in.at[j, source], d2_s.at[j, d - 1], d2_r.at[j, d - 1], at_z(d)
        ).wait_recv()

    def block(d):
        return rows(lax.rem(y + d, 4) * 96, 96)

    def d3_near(j, side):
        own = block(0)
        return copy(tok.at[j, own], tok.at[j, own], d3n_s.at[j, side], d3n_r.at[j, side], at_y(3 if side else 1))

    def d3_near_wait(j, side):
        source = block(1 if side else 3)
        copy(tok.at[j, source], tok.at[j, source], d3n_s.at[j, side], d3n_r.at[j, side], at_y(1)).wait_recv()

    def half_of(d, side):
        return pl.ds(pl.multiple_of(lax.rem(y + d, 4) * 96 + 48 * side, 48), 48)

    def d3_far(j, side):
        span = half_of(1 if side else 3, side)
        return copy(tok.at[j, span], tok.at[j, span], d3f_s.at[j, side], d3f_r.at[j, side], at_y(3 if side else 1))

    def d3_far_wait(j, side):
        span = half_of(2, side)
        copy(tok.at[j, span], tok.at[j, span], d3f_s.at[j, side], d3f_r.at[j, side], at_y(1)).wait_recv()

    def d_step(s, _):
        @pl.when(s < chunks)
        def _():
            j = s
            span = rows(j * CW, CW)
            moe_in = (hid[j] * scale * gain_ref[:, span]).astype(BF16)
            sent[j] = mm_tn(place, moe_in).astype(BF16)
            for d in (2, 1, 3):
                d1(j, d).start()
            d1_in[j, rows(x * 16, 16)] = sent[j, rows(x * 16, 16)]
            logits[...] += mm_nt(moe_in, router_ref[:, span])

        @pl.when((s >= 1) & (s < chunks + 1))
        def _():
            j = s - 1
            for d in (1, 2, 3):
                d1_wait(j, d)
            d2_out[j] = mm(q_ref[...], d1_in[j]).astype(BF16)
            for d in (4, 3, 5, 2, 6, 1, 7):
                d2(j, d).start()
            d2_in[j, rows(z * 16, 16)] = d2_out[j, rows(zl * 16, 16)]

        @pl.when((s >= 2) & (s < chunks + 2))
        def _():
            j = s - 2
            for d in range(1, 8):
                d2_wait(j, d)
            tok[j, block(0)] = mm(pack_ref[...], d2_in[j]).astype(BF16)
            d3_near(j, 0).start()
            d3_near(j, 1).start()

        @pl.when((s >= 3) & (s < chunks + 3))
        def _():
            j = s - 3
            for side in (0, 1):
                d3_near_wait(j, side)
                d3_far(j, side).start()

        @pl.when(s >= 4)
        def _():
            j = s - 4
            for side in (0, 1):
                d3_far_wait(j, side)
            tokens = tok[j]
            span = rows(j * CW, CW)
            for i in range(2):
                acc[i, 0] += mm_nt(tokens, wg[i, :, span])
                acc[i, 1] += mm_nt(tokens, wu[i, :, span])

        return 0

    for c in own_loads:
        c.wait()
    for c in swaps:
        c.wait_recv()
    lax.fori_loop(0, chunks + 4, d_step, 0)
    for i in range(2):
        gate = acc[i, 0]
        act[i] = (gate * jax.nn.sigmoid(gate) * acc[i, 1]).astype(BF16)

    @pl.loop(0, chunks)
    def _(j):
        for side in (0, 1):
            d3_near(j, side).wait_send()
            d3_far(j, side).wait_send()

    picked0 = jnp.sum(logits[...] * picks[0], axis=-1, keepdims=True)
    picked1 = jnp.sum(logits[...] * picks[1], axis=-1, keepdims=True)
    mix = jax.nn.sigmoid(picked0 - picked1) * hots[0] + jax.nn.sigmoid(picked1 - picked0) * hots[1]
    mix_hi = mix.astype(BF16)
    mix_lo = (mix - mix_hi.astype(F32)).astype(BF16)

    def f1(j):
        return ring_copies(j, tok, 96, f_opp, f_nb, fo_s, fo_r, fn_s, fn_r, at_y, y)

    def g2(j, d):
        to = rows(lax.rem(z + d, 8) * 16, 16)
        return copy(g2_out.at[j, to], g2_in.at[j, rows(z * 16, 16)], g2_s.at[j, d - 1], g2_r.at[j, d - 1], at_z(d))

    def g2_wait(j, d):
        source = rows(lax.rem(z + 8 - d, 8) * 16, 16)
        copy(
            g2_out.at[j, source], g2_in.at[j, source], g2_s.at[j, d - 1], g2_r.at[j, d - 1], at_z(d)
        ).wait_recv()

    def g3(j, d):
        to = rows(lax.rem(x + d, 4) * 16, 16)
        return copy(g3_out.at[j, to], g3_in.at[j, rows(x * 16, 16)], g3_s.at[j, d - 1], g3_r.at[j, d - 1], at_x(d))

    def g3_wait(j, d):
        source = rows(lax.rem(x + 4 - d, 4) * 16, 16)
        copy(
            g3_out.at[j, source], g3_in.at[j, source], g3_s.at[j, d - 1], g3_r.at[j, d - 1], at_x(d)
        ).wait_recv()

    def f_step(s, _):
        @pl.when(s < chunks)
        def _():
            j = s
            tok[j] = (mm(act[0], wd[0, :, rows(j * CW, CW)]) + mm(act[1], wd[1, :, rows(j * CW, CW)])).astype(BF16)
            copies = f1(j)
            copies[0].start()
            copies[1].start()

        @pl.when((s >= 1) & (s < chunks + 1))
        def _():
            j = s - 1
            ring_forward(j, tok, 96, f_opp, f1(j), y)

        @pl.when((s >= 2) & (s < chunks + 2))
        def _():
            j = s - 2
            total = ring_total(j, tok, 96, f_nb, f1(j), y).astype(BF16)
            g2_out[j] = mm(unpack_ref[...], total).astype(BF16)
            for d in (4, 3, 5, 2, 6, 1, 7):
                g2(j, d).start()
            g2_in[j, rows(z * 16, 16)] = g2_out[j, rows(z * 16, 16)]

        @pl.when((s >= 3) & (s < chunks + 3))
        def _():
            j = s - 3
            for d in range(1, 8):
                g2_wait(j, d)
            total = (g2_in[j, pl.ds(0, 64)].astype(F32) + g2_in[j, pl.ds(64, 64)].astype(F32)).astype(BF16)
            g3_out[j] = mm(qt_ref[...], total).astype(BF16)
            for d in (2, 1, 3):
                g3(j, d).start()
            g3_in[j, rows(x * 16, 16)] = g3_out[j, rows(x * 16, 16)]

        @pl.when(s >= 4)
        def _():
            j = s - 4
            for d in (1, 2, 3):
                g3_wait(j, d)
            back = g3_in[j]
            out_ref[:, rows(j * CW, CW)] = (hid[j] + mm(mix_hi, back) + mm(mix_lo, back)).astype(BF16)

        return 0

    lax.fori_loop(0, chunks + 4, f_step, 0)

    @pl.loop(0, chunks)
    def _(j):
        for c in c1(j) + f1(j):
            c.wait_send()
        for d in (1, 2, 3):
            c2(j, d).wait_send()
            d1(j, d).wait_send()
            g3(j, d).wait_send()
        for d in range(1, 8):
            d2(j, d).wait_send()
            g2(j, d).wait_send()
    for c in swaps + [state1, b_z()] + [state2(d) for d in (1, 2, 3)]:
        c.wait_send()
    for group in range(2):
        for side in range(2):
            b_near(group, side).wait_send()
            b_far(group, side).wait_send()
        for d in range(4):
            b_core(group, d).wait_send()

    @pl.when(zh == 0)
    def _():
        state3.wait_send()


def selections():
    q = np.zeros((64, 64), np.float32)
    pack = np.zeros((96, 128), np.float32)
    for e in range(4):
        for source in range(4):
            for s in range(3):
                q[e * 16 + source * 3 + s, source * 16 + e * 4 + s] = 1
    for source in range(8):
        for r in range(12):
            pack[source * 12 + r, source * 16 + r] = 1
    return tuple(jnp.asarray(a, BF16) for a in (q, q.T, pack, pack.T))


def shards(
    queries,
    keys_in,
    values_in,
    log_decay,
    attn_gain,
    out_weight,
    residual,
    moe_gain,
    router,
    gate_weight,
    up_weight,
    down_weight,
    routes,
):
    length, _, span = queries.shape
    count, _, width = residual.shape
    hidden = gate_weight.shape[2]
    n = width // CW
    flat = lambda a: a.reshape(length, span)
    dma = lambda *shape: pltpu.SemaphoreType.DMA(shape)
    vmem = lambda *shape: pltpu.VMEM(shape, BF16)
    scratch = [
        vmem(length, span), vmem(n, span, CW), pltpu.VMEM((2, length, HEAD), F32),
        vmem(2, 144, HEAD), vmem(2, 144, HEAD), vmem(4, 2, 144, HEAD), vmem(2, HEAD, HEAD), vmem(2, HEAD, HEAD),
        vmem(2, hidden, width), vmem(2, hidden, width), vmem(2, hidden, width),
        vmem(n, 256, CW), vmem(n, 2, 32, CW), vmem(n, 2, 64, CW), vmem(n, 64, CW), vmem(n, 3, 16, CW),
        pltpu.VMEM((n, 16, CW), F32), pltpu.VMEM((16, 128), F32),
        vmem(n, 64, CW), vmem(n, 64, CW), vmem(n, 64, CW), vmem(n, 128, CW), vmem(n, 384, CW),
        pltpu.VMEM((16, 16), F32), pltpu.VMEM((2, 2, 384, hidden), F32), vmem(2, 384, hidden),
        vmem(n, 2, 48, CW), vmem(n, 2, 96, CW), vmem(n, 128, CW), vmem(n, 128, CW), vmem(n, 64, CW), vmem(n, 64, CW),
        dma(4), dma(3), dma(3), pltpu.SemaphoreType.DMA, pltpu.SemaphoreType.DMA, dma(3), dma(3),
        pltpu.SemaphoreType.DMA, pltpu.SemaphoreType.DMA,
        dma(2, 4), dma(2, 4), pltpu.SemaphoreType.DMA, pltpu.SemaphoreType.DMA, dma(2, 2), dma(2, 2), dma(2, 2), dma(2, 2),
    ]
    for lanes in (2, 2, 3, 3, 7, 2, 2, 2, 2, 7, 3):
        scratch += [dma(n, lanes), dma(n, lanes)]
    in_vmem = pl.BlockSpec(memory_space=pltpu.VMEM)
    in_hbm = pl.BlockSpec(memory_space=pl.ANY)
    mixed = pl.pallas_call(
        block_kernel,
        out_shape=jax.ShapeDtypeStruct((count, width), BF16),
        in_specs=[in_vmem] * 5 + [in_hbm] + [in_vmem] * 8 + [in_hbm] * 3,
        out_specs=in_vmem,
        scratch_shapes=scratch,
        compiler_params=pltpu.CompilerParams(collective_id=0, has_side_effects=True, vmem_limit_bytes=67043328),
    )(
        flat(queries), flat(keys_in), flat(values_in), log_decay.reshape(-1, length), attn_gain.reshape(1, span),
        out_weight, residual.reshape(count, width), moe_gain.reshape(1, width), router.T, routes.reshape(count, 2),
        *selections(), jnp.swapaxes(gate_weight, 1, 2), jnp.swapaxes(up_weight, 1, 2), down_weight,
    )
    return mixed.reshape(residual.shape)


def solution(mesh):
    return jax.shard_map(
        shards,
        mesh=mesh,
        in_specs=(
            P("ctx", None, "ep"),
            P("ctx", None, "ep"),
            P("ctx", None, "ep"),
            P("ep", None, "ctx"),
            P("ep"),
            P("ep", "ctx"),
            P(("ctx", "ep"), None, None),
            P(),
            P(),
            P("ep", None, "ctx"),
            P("ep", None, "ctx"),
            P("ep", "ctx", None),
            P(("ctx", "ep"), None, None),
        ),
        out_specs=P(("ctx", "ep"), None, None),
        check_vma=False,
    )
```

```python
import jax
import jax.numpy as jnp
import numpy as np
from jax import lax
from jax.experimental import pallas as pl
from jax.experimental.pallas import tpu as pltpu
from jax.sharding import PartitionSpec as P

MESH = pl.DeviceIdType.MESH
F32, BF16 = jnp.float32, jnp.bfloat16
CW = 512
HW = CW // 2
HEAD = 128


def silu_float(values):
    return values * jax.nn.sigmoid(values)


def place_of():
    ctx, ep = lax.axis_index("ctx"), lax.axis_index("ep")
    y, core = lax.rem(ctx, 8) // 2, lax.rem(ctx, 2)
    z = (ctx // 8) * 4 + lax.rem(ep, 4)
    return ep // 4, y, z, core


def device_at(x, y, z, core):
    return ((z // 4) * 8 + y * 2 + core, x * 4 + lax.rem(z, 4))


def mm(a, b):
    return jnp.dot(a, b, preferred_element_type=F32)


def mm_nt(a, b, precision=None):
    return lax.dot_general(a, b, (((1,), (1,)), ((), ())), precision=precision, preferred_element_type=F32)


def mm_tn(a, b, precision=None):
    return lax.dot_general(a, b, (((0,), (0,)), ((), ())), precision=precision, preferred_element_type=F32)


def rows(start, size):
    return pl.ds(pl.multiple_of(start, size), size)


def block_kernel(
    queries, keys, values, decay_ref, head_gain, ow_hbm, res_ref, gain_ref, router_ref, routes_ref,
    q_ref, qt_ref, pack_ref, unpack_ref, gate_hbm, up_hbm, down_hbm,
    out_ref,
    nh, wo, inside, s1_out, s1_in, s2, s3_out, s3_in,
    wg, wu, wd, part, c1_opp, c1_nb, c2_out, c2_in, hid, ssq, rowsq, sent, d1_in, d2_out, d2_in, tok, logits,
    acc, act, f_opp, f_nb, g2_out, g2_in, g3_out, g3_in,
    load_sem, swap_s, swap_r, s1_s, s1_r, s2_s, s2_r, s3_s, s3_r,
    bc_s, bc_r, bz_s, bz_r, bn_s, bn_r, bf_s, bf_r,
    c1o_s, c1o_r, c1n_s, c1n_r, c2_s, c2_r, d1_s, d1_r, d2_s, d2_r, d3n_s, d3n_r, d3f_s, d3f_r,
    fo_s, fo_r, fn_s, fn_r, g2_s, g2_r, g3_s, g3_r,
):
    x, y, z, core = place_of()
    zl, zh = lax.rem(z, 4), z // 4
    chunks = hid.shape[0]

    def at_x(d):
        return device_at(lax.rem(x + d, 4), y, z, core)

    def at_y(d):
        return device_at(x, lax.rem(y + d, 4), z, core)

    def at_z(d):
        return device_at(x, y, lax.rem(z + d, 8), core)

    def at_line(d):
        return device_at(x, y, zh * 4 + lax.rem(zl + d, 4), core)

    def copy(src, dst, send, recv, to):
        return pltpu.make_async_remote_copy(
            src_ref=src, dst_ref=dst, send_sem=send, recv_sem=recv, device_id=to, device_id_type=MESH
        )

    twin = device_at(x, y, z, 1 - core)
    barrier = pltpu.get_barrier_semaphore()
    peers = [twin] + [at_x(d) for d in (1, 2, 3)] + [at_y(d) for d in (1, 2, 3)] + [at_z(d) for d in range(1, 8)]
    for peer in peers:
        pl.semaphore_signal(barrier, inc=1, device_id=peer, device_id_type=MESH)
    weights = ((gate_hbm.at[0], wg), (up_hbm.at[0], wu), (down_hbm.at[0], wd))
    own_loads = [pltpu.make_async_copy(w, to.at[0], load_sem.at[i]) for i, (w, to) in enumerate(weights)]
    swaps = [copy(w, to.at[1], swap_s.at[i], swap_r.at[i], twin) for i, (w, to) in enumerate(weights)]
    ssq[...] = jnp.zeros_like(ssq)
    rowsq[...] = jnp.zeros_like(rowsq)
    logits[...] = jnp.zeros_like(logits)
    acc[...] = jnp.zeros_like(acc)

    length = queries.shape[0]
    at_t = lax.broadcasted_iota(jnp.int32, (length, length), 0)
    at_u = lax.broadcasted_iota(jnp.int32, (length, length), 1)
    highest = lax.Precision.HIGHEST
    own_state, own_decay, cumulative = [], [], []
    for h in range(2):
        lanes = pl.ds(h * HEAD, HEAD)
        log_row = decay_ref[h]
        log_col = jnp.sum(jnp.where(at_u == at_t, log_row, 0.0), axis=1, keepdims=True)
        cum_col = jnp.sum(jnp.where(at_u <= at_t, log_row, 0.0), axis=1, keepdims=True)
        cum_row = jnp.sum(jnp.where(at_t <= at_u, log_col, 0.0), axis=0, keepdims=True)
        last = jnp.sum(log_row, axis=1, keepdims=True)
        k = silu_float(keys[:, lanes].astype(F32))
        own_state.append(mm_tn(k * jnp.exp(last - cum_col), values[:, lanes].astype(F32), highest))
        own_decay.append(jnp.broadcast_to(jnp.exp(last), (1, HEAD)))
        cumulative.append((cum_col, cum_row))

    def write_state(to, h, state, decay):
        high = decay.astype(BF16)
        low = (decay - high.astype(F32)).astype(BF16)
        first = lax.broadcasted_iota(jnp.int32, (16, HEAD), 0) == 0
        to[h, pl.ds(0, HEAD)] = state.astype(BF16)
        to[h, pl.ds(HEAD, 16)] = jnp.where(first, high.astype(F32), low.astype(F32)).astype(BF16)

    def read_state(of, h):
        tail = of[h, pl.ds(HEAD, 16)].astype(F32)
        return of[h, pl.ds(0, HEAD)].astype(F32), tail[0:1, :] + tail[1:2, :]

    for h in range(2):
        write_state(s1_out, h, own_state[h], own_decay[h])
    for h in range(2):
        lanes = pl.ds(h * HEAD, HEAD)
        cum_col, cum_row = cumulative[h]
        q = silu_float(queries[:, lanes].astype(F32))
        k = silu_float(keys[:, lanes].astype(F32))
        causal = at_t >= at_u
        damping = jnp.where(causal, jnp.exp(jnp.where(causal, cum_col - cum_row, 0.0)), 0.0)
        scores = mm_nt(q, k, highest) * damping
        inside[h] = jnp.dot(scores, values[:, lanes].astype(F32), precision=highest, preferred_element_type=F32)

    count, number = routes_ref.shape[1], router_ref.shape[0]
    expert = lax.broadcasted_iota(jnp.int32, (count, number), 1)
    token = lax.broadcasted_iota(jnp.int32, (count, count), 0)
    after = lax.broadcasted_iota(jnp.int32, (count, count), 1)
    named = [
        jnp.sum(jnp.where(token == after, routes_ref[r : r + 1, :], 0), axis=1, keepdims=True) for r in (0, 1)
    ]
    picks = [(named[r] == expert).astype(F32) for r in (0, 1)]
    earlier = token > after
    taken = mm(earlier.astype(F32).astype(BF16), (picks[0] + picks[1]).astype(BF16))
    slot = lax.broadcasted_iota(jnp.int32, (count, 4 * number), 1)
    hots = []
    for r in (0, 1):
        used = jnp.sum(taken * picks[r], axis=-1, keepdims=True).astype(jnp.int32)
        hots.append((named[r] * 4 + used == slot).astype(F32))
    place = (hots[0] + hots[1]).astype(BF16)

    pl.semaphore_wait(barrier, len(peers))
    state1 = copy(s1_out, s1_in, s1_s, s1_r, twin)
    state1.start()


    def columns(group, d, of_core):
        chip = lax.rem(zh + group, 2) * 4 + lax.rem(y + d, 4)
        return pl.ds(pl.multiple_of((chip * 2 + of_core) * 384, 128), 384)

    def b_core(group, d):
        src = wo.at[:, columns(group, d, core)]
        return copy(ow_hbm if (group, d) == (0, 0) else src, src, bc_s.at[group, d], bc_r.at[group, d], twin)

    def b_core_wait(group, d):
        to = wo.at[:, columns(group, d, 1 - core)]
        copy(to, to, bc_s.at[group, d], bc_r.at[group, d], twin).wait_recv()

    def b_z():
        return copy(ow_hbm, wo.at[:, columns(0, 0, core)], bz_s, bz_r, at_z(4))

    def b_z_wait():
        to = wo.at[:, columns(1, 0, core)]
        copy(to, to, bz_s, bz_r, at_z(4)).wait_recv()

    def b_near(group, side):
        src = wo.at[:, columns(group, 0, core)]
        return copy(
            ow_hbm if group == 0 else src, src, bn_s.at[group, side], bn_r.at[group, side], at_y(3 if side else 1)
        )

    def b_near_wait(group, side):
        to = wo.at[:, columns(group, 1 if side else 3, core)]
        copy(to, to, bn_s.at[group, side], bn_r.at[group, side], at_y(1)).wait_recv()

    def b_far(group, side):
        to = wo.at[pl.ds(128 * side, 128), columns(group, 1 if side else 3, core)]
        return copy(to, to, bf_s.at[group, side], bf_r.at[group, side], at_y(3 if side else 1))

    def b_far_wait(group, side):
        to = wo.at[pl.ds(128 * side, 128), columns(group, 2, core)]
        copy(to, to, bf_s.at[group, side], bf_r.at[group, side], at_y(1)).wait_recv()

    def b_first(group):
        for side in (0, 1):
            b_near_wait(group, side)
            b_far(group, side).start()
            b_core(group, 1 if side else 3).start()

    def b_second(group):
        b_far_wait(group, 0)
        b_far_wait(group, 1)
        b_core(group, 2).start()

    own_columns = pltpu.make_async_copy(ow_hbm, wo.at[:, columns(0, 0, core)], load_sem.at[3])
    own_columns.start()
    b_z().start()
    b_near(0, 0).start()
    b_near(0, 1).start()
    b_core(0, 0).start()
    for c in own_loads:
        c.start()

    state1.wait_recv()
    first_core = core == 0
    twin_state = []
    for h in range(2):
        state, decay = read_state(s1_in, h)
        twin_state.append((state, decay))
        chip_state = jnp.where(
            first_core, decay * own_state[h] + state, own_decay[h] * state + own_state[h]
        )
        write_state(s2.at[y], h, chip_state, own_decay[h] * decay)

    def state2(d):
        return copy(s2.at[y], s2.at[y], s2_s.at[d - 1], s2_r.at[d - 1], at_y(d))

    for d in (2, 1, 3):
        state2(d).start()
    b_first(0)
    b_z_wait()
    b_near(1, 0).start()
    b_near(1, 1).start()
    b_core(1, 0).start()
    for d in (1, 2, 3):
        source = s2.at[lax.rem(y + 4 - d, 4)]
        copy(source, source, s2_s.at[d - 1], s2_r.at[d - 1], at_y(d)).wait_recv()
    entering = []
    for h in range(2):
        total = jnp.zeros((HEAD, HEAD), F32)
        before = jnp.zeros((HEAD, HEAD), F32)
        factor = jnp.ones((1, HEAD), F32)
        for other in range(4):
            state, decay = read_state(s2.at[other], h)
            before = jnp.where(other == y, total, before)
            factor = jnp.where(other < y, factor * decay, factor)
            total = decay * total + state
        s3_out[h] = total.astype(BF16)
        entering.append((before, factor))
    state3 = copy(s3_out, s3_in, s3_s, s3_r, at_z(4))

    @pl.when(zh == 0)
    def _():
        state3.start()
        s3_in[...] = jnp.zeros_like(s3_in)

    b_second(0)
    b_first(1)

    @pl.when(zh == 1)
    def _():
        state3.wait_recv()

    for h in range(2):
        lanes = pl.ds(h * HEAD, HEAD)
        before, factor = entering[h]
        state, decay = twin_state[h]
        prefix = factor * s3_in[h].astype(F32) + before
        prefix = jnp.where(first_core, prefix, decay * prefix + state)
        q = silu_float(queries[:, lanes].astype(F32))
        carried = jnp.dot(q, prefix, precision=highest, preferred_element_type=F32)
        heads_out = inside[h] + jnp.exp(cumulative[h][0]) * carried
        mean_square = jnp.mean(heads_out * heads_out, axis=-1, keepdims=True)
        nh[:, lanes] = (heads_out * lax.rsqrt(mean_square + 1e-06) * head_gain[:, lanes]).astype(BF16)
    b_second(1)
    own_columns.wait()
    for group in range(2):
        for d in range(4):
            b_core_wait(group, d)

    def ring_copies(j, buf, size, opp, near, so, ro, sn, rn, at, mine):
        half = size // 2
        far_a = pl.ds(pl.multiple_of(lax.rem(mine + 2, 4) * size, size), half)
        far_b = pl.ds(pl.multiple_of(lax.rem(mine + 2, 4) * size + half, half), half)
        right = rows(lax.rem(mine + 1, 4) * size, size)
        left = rows(lax.rem(mine + 3, 4) * size, size)
        return (
            copy(buf.at[j, far_a], opp.at[j, 0], so.at[j, 0], ro.at[j, 0], at(1)),
            copy(buf.at[j, far_b], opp.at[j, 1], so.at[j, 1], ro.at[j, 1], at(3)),
            copy(buf.at[j, right], near.at[j, 0], sn.at[j, 0], rn.at[j, 0], at(1)),
            copy(buf.at[j, left], near.at[j, 1], sn.at[j, 1], rn.at[j, 1], at(3)),
        )

    def ring_forward(j, buf, size, opp, copies, mine):
        half = size // 2
        copies[0].wait_recv()
        to_right = pl.ds(pl.multiple_of(lax.rem(mine + 1, 4) * size, size), half)
        buf[j, to_right] = (buf[j, to_right].astype(F32) + opp[j, 0].astype(F32)).astype(BF16)
        copies[2].start()
        copies[1].wait_recv()
        to_left = pl.ds(pl.multiple_of(lax.rem(mine + 3, 4) * size + half, half), half)
        buf[j, to_left] = (buf[j, to_left].astype(F32) + opp[j, 1].astype(F32)).astype(BF16)
        copies[3].start()

    def ring_total(j, buf, size, near, copies, mine):
        copies[2].wait_recv()
        copies[3].wait_recv()
        own = rows(mine * size, size)
        return buf[j, own].astype(F32) + near[j, 0].astype(F32) + near[j, 1].astype(F32)

    def c1(j):
        return ring_copies(j, part, 64, c1_opp, c1_nb, c1o_s, c1o_r, c1n_s, c1n_r, at_x, x)

    def c2(j, d):
        to = rows(lax.rem(zl + d, 4) * 16, 16)
        return copy(c2_out.at[j, to], c2_in.at[j, d - 1], c2_s.at[j, d - 1], c2_r.at[j, d - 1], at_line(d))

    def d1(j, d):
        to = rows(lax.rem(x + d, 4) * 16, 16)
        return copy(sent.at[j, to], d1_in.at[j, rows(x * 16, 16)], d1_s.at[j, d - 1], d1_r.at[j, d - 1], at_x(d))

    def d1_wait(j, d):
        source = rows(lax.rem(x + 4 - d, 4) * 16, 16)
        copy(sent.at[j, source], d1_in.at[j, source], d1_s.at[j, d - 1], d1_r.at[j, d - 1], at_x(d)).wait_recv()

    def d2(j, d):
        to = rows(lax.rem(zl + d, 4) * 24, 24)
        return copy(d2_out.at[j, to], d2_in.at[j, rows(z * 24, 24)], d2_s.at[j, d - 1], d2_r.at[j, d - 1], at_z(d))

    def d2_wait(j, d):
        source = rows(lax.rem(z + 8 - d, 8) * 24, 24)
        copy(
            d2_out.at[j, pl.ds(0, 24)], d2_in.at[j, source], d2_s.at[j, d - 1], d2_r.at[j, d - 1], at_z(d)
        ).wait_recv()

    def block(d):
        return rows(lax.rem(y + d, 4) * 96, 96)

    def d3_near(j, side):
        own = block(0)
        return copy(tok.at[j, own], tok.at[j, own], d3n_s.at[j, side], d3n_r.at[j, side], at_y(3 if side else 1))

    def d3_near_wait(j, side):
        source = block(1 if side else 3)
        copy(tok.at[j, source], tok.at[j, source], d3n_s.at[j, side], d3n_r.at[j, side], at_y(1)).wait_recv()

    def half_of(d, side):
        return pl.ds(pl.multiple_of(lax.rem(y + d, 4) * 96 + 48 * side, 48), 48)

    def d3_far(j, side):
        span = half_of(1 if side else 3, side)
        return copy(tok.at[j, span], tok.at[j, span], d3f_s.at[j, side], d3f_r.at[j, side], at_y(3 if side else 1))

    def d3_far_wait(j, side):
        span = half_of(2, side)
        copy(tok.at[j, span], tok.at[j, span], d3f_s.at[j, side], d3f_r.at[j, side], at_y(1)).wait_recv()

    def stage(s, skew, body):
        pl.when((s >= skew) & (s < chunks + skew))(lambda: body(s - skew))

    def project(j):
        part[j] = mm(nh[...], wo[:, rows(j * CW, CW)]).astype(BF16)
        copies = c1(j)
        copies[0].start()
        copies[1].start()

    def project_line(j):
        c2_out[j] = ring_total(j, part, 64, c1_nb, c1(j), x).astype(BF16)
        for d in (3, 2, 1):
            c2(j, d).start()

    def dispatch(j):
        span = rows(j * CW, CW)
        total = c2_out[j, rows(zl * 16, 16)].astype(F32)
        for d in (1, 2, 3):
            c2(j, d).wait_recv()
            total = total + c2_in[j, d - 1].astype(F32)
        state = res_ref[:, span].astype(F32) + total
        gained = (state * gain_ref[:, span]).astype(BF16)
        sent[j] = mm_tn(place, gained).astype(BF16)
        for d in (2, 1, 3):
            d1(j, d).start()
        d1_in[j, rows(x * 16, 16)] = sent[j, rows(x * 16, 16)]
        hid[j] = state
        ssq[...] += jnp.sum(state * state, axis=-1, keepdims=True)
        logits[...] += mm_nt(gained, router_ref[:, span])

    def dispatch_z(j):
        for d in (1, 2, 3):
            d1_wait(j, d)
        d2_out[j] = (mm(q_ref[0], d1_in[j, :, pl.ds(0, HW)]) + mm(q_ref[1], d1_in[j, :, pl.ds(HW, HW)])).astype(BF16)
        for d in (4, 3, 5, 2, 6, 1, 7):
            d2(j, d).start()
        d2_in[j, rows(z * 24, 24)] = d2_out[j, rows(zl * 24, 24)]

    def gather_near(j):
        for d in range(1, 8):
            d2_wait(j, d)
        arrived = d2_in[j]
        tok[j, block(0), pl.ds(0, HW)] = mm(pack_ref[0], arrived).astype(BF16)
        tok[j, block(0), pl.ds(HW, HW)] = mm(pack_ref[1], arrived).astype(BF16)
        d3_near(j, 0).start()
        d3_near(j, 1).start()

    def gather_far(j):
        for side in (0, 1):
            d3_near_wait(j, side)
            d3_far(j, side).start()

    def multiply(j):
        for side in (0, 1):
            d3_far_wait(j, side)

        @pl.when(j == 0)
        def _():
            swaps[0].wait_recv()
            swaps[1].wait_recv()

        span = rows(j * CW, CW)
        tokens = tok[j]
        for i in range(2):
            acc[i, 0] += mm_nt(tokens, wg[i, :, span])
            acc[i, 1] += mm_nt(tokens, wu[i, :, span])
        plain = tokens.astype(F32) * (1.0 / gain_ref[:, span])
        square = plain * plain
        rowsq[...] += sum(square[:, k * 128 : (k + 1) * 128] for k in range(CW // 128))

    def cd_step(s, _):
        stage(s, 0, project)
        stage(s, 1, lambda j: ring_forward(j, part, 64, c1_opp, c1(j), x))
        stage(s, 2, project_line)
        stage(s, 4, dispatch)
        stage(s, 5, dispatch_z)
        stage(s, 7, gather_near)
        stage(s, 8, gather_far)
        stage(s, 9, multiply)
        return 0

    for c in swaps:
        c.start()
    for c in own_loads:
        c.wait()
    lax.fori_loop(0, chunks + 9, cd_step, 0)
    swaps[2].wait_recv()
    per_width = 1.0 / (chunks * CW)
    scale = lax.rsqrt(jnp.sum(rowsq[...], axis=-1, keepdims=True) * per_width + 1e-06)
    for i in range(2):
        gate = acc[i, 0] * scale
        act[i] = (gate * jax.nn.sigmoid(gate) * (acc[i, 1] * scale)).astype(BF16)

    @pl.loop(0, chunks)
    def _(j):
        for side in (0, 1):
            d3_near(j, side).wait_send()
            d3_far(j, side).wait_send()

    router_out = logits[...] * lax.rsqrt(ssq[:, 0:1] * per_width + 1e-06)
    picked0 = jnp.sum(router_out * picks[0], axis=-1, keepdims=True)
    picked1 = jnp.sum(router_out * picks[1], axis=-1, keepdims=True)
    mix = jax.nn.sigmoid(picked0 - picked1) * hots[0] + jax.nn.sigmoid(picked1 - picked0) * hots[1]
    mix_hi = mix.astype(BF16)
    mix_lo = (mix - mix_hi.astype(F32)).astype(BF16)

    def f1(j):
        return ring_copies(j, tok, 96, f_opp, f_nb, fo_s, fo_r, fn_s, fn_r, at_y, y)

    def g2(j, d):
        to = rows(lax.rem(z + d, 8) * 24, 24)
        return copy(g2_out.at[j, to], g2_in.at[j, rows(z * 24, 24)], g2_s.at[j, d - 1], g2_r.at[j, d - 1], at_z(d))

    def g2_wait(j, d):
        source = rows(lax.rem(z + 8 - d, 8) * 24, 24)
        copy(
            g2_out.at[j, source], g2_in.at[j, source], g2_s.at[j, d - 1], g2_r.at[j, d - 1], at_z(d)
        ).wait_recv()

    def g3(j, d):
        to = rows(lax.rem(x + d, 4) * 16, 16)
        return copy(g3_out.at[j, to], g3_in.at[j, rows(x * 16, 16)], g3_s.at[j, d - 1], g3_r.at[j, d - 1], at_x(d))

    def g3_wait(j, d):
        source = rows(lax.rem(x + 4 - d, 4) * 16, 16)
        copy(
            g3_out.at[j, source], g3_in.at[j, source], g3_s.at[j, d - 1], g3_r.at[j, d - 1], at_x(d)
        ).wait_recv()

    def down(j):
        span = rows(j * CW, CW)
        tok[j] = (mm(act[0], wd[0, :, span]) + mm(act[1], wd[1, :, span])).astype(BF16)
        copies = f1(j)
        copies[0].start()
        copies[1].start()

    def return_z(j):
        total = ring_total(j, tok, 96, f_nb, f1(j), y).astype(BF16)
        g2_out[j] = (mm(unpack_ref[0], total[:, :HW]) + mm(unpack_ref[1], total[:, HW:])).astype(BF16)
        for d in (4, 3, 5, 2, 6, 1, 7):
            g2(j, d).start()
        g2_in[j, rows(z * 24, 24)] = g2_out[j, rows(z * 24, 24)]

    def return_x(j):
        for d in range(1, 8):
            g2_wait(j, d)
        total = (g2_in[j, pl.ds(0, 96)].astype(F32) + g2_in[j, pl.ds(96, 96)].astype(F32)).astype(BF16)
        g3_out[j, :, pl.ds(0, HW)] = mm(qt_ref[0], total).astype(BF16)
        g3_out[j, :, pl.ds(HW, HW)] = mm(qt_ref[1], total).astype(BF16)
        for d in (2, 1, 3):
            g3(j, d).start()
        g3_in[j, rows(x * 16, 16)] = g3_out[j, rows(x * 16, 16)]

    def combine(j):
        for d in (1, 2, 3):
            g3_wait(j, d)
        back = g3_in[j]
        out_ref[:, rows(j * CW, CW)] = (hid[j] + mm(mix_hi, back) + mm(mix_lo, back)).astype(BF16)

    def f_step(s, _):
        stage(s, 0, down)
        stage(s, 2, lambda j: ring_forward(j, tok, 96, f_opp, f1(j), y))
        stage(s, 4, return_z)
        stage(s, 6, return_x)
        stage(s, 7, combine)
        return 0

    lax.fori_loop(0, chunks + 7, f_step, 0)

    @pl.loop(0, chunks)
    def _(j):
        for c in c1(j) + f1(j):
            c.wait_send()
        for d in (1, 2, 3):
            c2(j, d).wait_send()
            d1(j, d).wait_send()
            g3(j, d).wait_send()
        for d in range(1, 8):
            d2(j, d).wait_send()
            g2(j, d).wait_send()
    for c in swaps + [state1, b_z()] + [state2(d) for d in (1, 2, 3)]:
        c.wait_send()
    for group in range(2):
        for side in range(2):
            b_near(group, side).wait_send()
            b_far(group, side).wait_send()
        for d in range(4):
            b_core(group, d).wait_send()

    @pl.when(zh == 0)
    def _():
        state3.wait_send()


def selections():
    q = np.zeros((2, 96, 64), np.float32)
    pack = np.zeros((2, 96, 192), np.float32)
    for half in range(2):
        for e in range(4):
            for source in range(4):
                for s in range(3):
                    q[half, e * 24 + half * 12 + source * 3 + s, source * 16 + e * 4 + s] = 1
        for source in range(8):
            for r in range(12):
                pack[half, source * 12 + r, source * 24 + half * 12 + r] = 1
    return tuple(jnp.asarray(a, BF16) for a in (q, q.transpose(0, 2, 1), pack, pack.transpose(0, 2, 1)))


def shards(
    queries,
    keys_in,
    values_in,
    log_decay,
    attn_gain,
    out_weight,
    residual,
    moe_gain,
    router,
    gate_weight,
    up_weight,
    down_weight,
    routes,
):
    length, _, span = queries.shape
    count, _, width = residual.shape
    hidden = gate_weight.shape[2]
    n = width // CW
    flat = lambda a: a.reshape(length, span)
    dma = lambda *shape: pltpu.SemaphoreType.DMA(shape)
    vmem = lambda *shape: pltpu.VMEM(shape, BF16)
    scratch = [
        vmem(length, span), vmem(span, width), pltpu.VMEM((2, length, HEAD), F32),
        vmem(2, 144, HEAD), vmem(2, 144, HEAD), vmem(4, 2, 144, HEAD), vmem(2, HEAD, HEAD), vmem(2, HEAD, HEAD),
        vmem(2, hidden, width), vmem(2, hidden, width), vmem(2, hidden, width),
        vmem(n, 256, CW), vmem(n, 2, 32, CW), vmem(n, 2, 64, CW), vmem(n, 64, CW), vmem(n, 3, 16, CW),
        pltpu.VMEM((n, 16, CW), F32), pltpu.VMEM((16, 128), F32), pltpu.VMEM((384, 128), F32),
        vmem(n, 64, CW), vmem(n, 64, CW), vmem(n, 96, HW), vmem(n, 192, HW), vmem(n, 384, CW),
        pltpu.VMEM((16, 16), F32), pltpu.VMEM((2, 2, 384, hidden), F32), vmem(2, 384, hidden),
        vmem(n, 2, 48, CW), vmem(n, 2, 96, CW), vmem(n, 192, HW), vmem(n, 192, HW), vmem(n, 64, CW), vmem(n, 64, CW),
        dma(4), dma(3), dma(3), pltpu.SemaphoreType.DMA, pltpu.SemaphoreType.DMA, dma(3), dma(3),
        pltpu.SemaphoreType.DMA, pltpu.SemaphoreType.DMA,
        dma(2, 4), dma(2, 4), pltpu.SemaphoreType.DMA, pltpu.SemaphoreType.DMA, dma(2, 2), dma(2, 2), dma(2, 2), dma(2, 2),
    ]
    for lanes in (2, 2, 3, 3, 7, 2, 2, 2, 2, 7, 3):
        scratch += [dma(n, lanes), dma(n, lanes)]
    in_vmem = pl.BlockSpec(memory_space=pltpu.VMEM)
    in_hbm = pl.BlockSpec(memory_space=pl.ANY)
    mixed = pl.pallas_call(
        block_kernel,
        out_shape=jax.ShapeDtypeStruct((count, width), BF16),
        in_specs=[in_vmem] * 5 + [in_hbm] + [in_vmem] * 8 + [in_hbm] * 3,
        out_specs=in_vmem,
        scratch_shapes=scratch,
        compiler_params=pltpu.CompilerParams(collective_id=0, has_side_effects=True, vmem_limit_bytes=67043328),
    )(
        flat(queries), flat(keys_in), flat(values_in), log_decay, attn_gain.reshape(1, span),
        out_weight, residual.reshape(count, width), moe_gain.reshape(1, width), router.T, routes.reshape(count, 2).T,
        *selections(), jnp.swapaxes(gate_weight, 1, 2), jnp.swapaxes(up_weight, 1, 2), down_weight,
    )
    return mixed.reshape(residual.shape)


def solution(mesh):
    return jax.shard_map(
        shards,
        mesh=mesh,
        in_specs=(
            P("ctx", None, "ep"),
            P("ctx", None, "ep"),
            P("ctx", None, "ep"),
            P("ep", None, "ctx"),
            P("ep"),
            P("ep", "ctx"),
            P(("ctx", "ep"), None, None),
            P(),
            P(),
            P("ep", None, "ctx"),
            P("ep", None, "ctx"),
            P("ep", "ctx", None),
            P(("ctx", "ep"), None, None),
        ),
        out_specs=P(("ctx", "ep"), None, None),
        check_vma=False,
    )
```

```python
import jax
import jax.numpy as jnp
import numpy as np
from jax import lax
from jax.experimental import pallas as pl
from jax.experimental.pallas import tpu as pltpu
from jax.sharding import PartitionSpec as P

MESH = pl.DeviceIdType.MESH
F32, BF16 = jnp.float32, jnp.bfloat16
CW = 768
HW = CW // 2
HEAD = 128


def silu_float(values):
    return values * jax.nn.sigmoid(values)


def place_of():
    ctx, ep = lax.axis_index("ctx"), lax.axis_index("ep")
    y, core = lax.rem(ctx, 8) // 2, lax.rem(ctx, 2)
    z = (ctx // 8) * 4 + lax.rem(ep, 4)
    return ep // 4, y, z, core


def device_at(x, y, z, core):
    return ((z // 4) * 8 + y * 2 + core, x * 4 + lax.rem(z, 4))


def mm(a, b):
    return jnp.dot(a, b, preferred_element_type=F32)


def mm_nt(a, b, precision=None):
    return lax.dot_general(a, b, (((1,), (1,)), ((), ())), precision=precision, preferred_element_type=F32)


def mm_tn(a, b, precision=None):
    return lax.dot_general(a, b, (((0,), (0,)), ((), ())), precision=precision, preferred_element_type=F32)


def rows(start, size):
    return pl.ds(pl.multiple_of(start, size), size)


def block_kernel(
    queries, keys, values, decay_ref, head_gain, ow_hbm, res_ref, gain_ref, router_ref, routes_ref,
    q_ref, qt_ref, pack_ref, unpack_ref, gate_hbm, up_hbm, down_hbm,
    out_ref,
    nh, wo, inside, s1_out, s1_in, s2, s3_out, s3_in,
    wg, wu, wd, part, c1_opp, c1_nb, c2_out, c2_in, hid, ssq, rowsq, sent, d1_in, d2_out, d2_in, tok, logits,
    acc, act, f_opp, f_nb, g2_out, g2_in, g3_out, g3_in,
    load_sem, swap_s, swap_r, s1_s, s1_r, s2_s, s2_r, s3_s, s3_r,
    bc_s, bc_r, bz_s, bz_r, bn_s, bn_r, bf_s, bf_r,
    c1o_s, c1o_r, c1n_s, c1n_r, c2_s, c2_r, d1_s, d1_r, d2_s, d2_r, d3n_s, d3n_r, d3f_s, d3f_r,
    fo_s, fo_r, fn_s, fn_r, g2_s, g2_r, g3_s, g3_r,
):
    x, y, z, core = place_of()
    zl, zh = lax.rem(z, 4), z // 4
    chunks = hid.shape[0]

    def at_x(d):
        return device_at(lax.rem(x + d, 4), y, z, core)

    def at_y(d):
        return device_at(x, lax.rem(y + d, 4), z, core)

    def at_z(d):
        return device_at(x, y, lax.rem(z + d, 8), core)

    def at_line(d):
        return device_at(x, y, zh * 4 + lax.rem(zl + d, 4), core)

    def copy(src, dst, send, recv, to):
        return pltpu.make_async_remote_copy(
            src_ref=src, dst_ref=dst, send_sem=send, recv_sem=recv, device_id=to, device_id_type=MESH
        )

    twin = device_at(x, y, z, 1 - core)
    barrier = pltpu.get_barrier_semaphore()
    peers = [twin] + [at_x(d) for d in (1, 2, 3)] + [at_y(d) for d in (1, 2, 3)] + [at_z(d) for d in range(1, 8)]
    for peer in peers:
        pl.semaphore_signal(barrier, inc=1, device_id=peer, device_id_type=MESH)
    weights = ((gate_hbm.at[0], wg), (up_hbm.at[0], wu), (down_hbm.at[0], wd))
    own_loads = [pltpu.make_async_copy(w, to.at[0], load_sem.at[i]) for i, (w, to) in enumerate(weights)]
    swaps = [copy(w, to.at[1], swap_s.at[i], swap_r.at[i], twin) for i, (w, to) in enumerate(weights)]
    ssq[...] = jnp.zeros_like(ssq)
    rowsq[...] = jnp.zeros_like(rowsq)
    logits[...] = jnp.zeros_like(logits)
    acc[...] = jnp.zeros_like(acc)

    length = queries.shape[0]
    at_t = lax.broadcasted_iota(jnp.int32, (length, length), 0)
    at_u = lax.broadcasted_iota(jnp.int32, (length, length), 1)
    highest = lax.Precision.HIGHEST
    own_state, own_decay, cumulative = [], [], []
    for h in range(2):
        lanes = pl.ds(h * HEAD, HEAD)
        log_row = decay_ref[h]
        log_col = jnp.sum(jnp.where(at_u == at_t, log_row, 0.0), axis=1, keepdims=True)
        cum_col = jnp.sum(jnp.where(at_u <= at_t, log_row, 0.0), axis=1, keepdims=True)
        cum_row = jnp.sum(jnp.where(at_t <= at_u, log_col, 0.0), axis=0, keepdims=True)
        last = jnp.sum(log_row, axis=1, keepdims=True)
        k = silu_float(keys[:, lanes].astype(F32))
        own_state.append(mm_tn(k * jnp.exp(last - cum_col), values[:, lanes].astype(F32), highest))
        own_decay.append(jnp.broadcast_to(jnp.exp(last), (1, HEAD)))
        cumulative.append((cum_col, cum_row))

    def write_state(to, h, state, decay):
        high = decay.astype(BF16)
        low = (decay - high.astype(F32)).astype(BF16)
        first = lax.broadcasted_iota(jnp.int32, (16, HEAD), 0) == 0
        to[h, pl.ds(0, HEAD)] = state.astype(BF16)
        to[h, pl.ds(HEAD, 16)] = jnp.where(first, high.astype(F32), low.astype(F32)).astype(BF16)

    def read_state(of, h):
        tail = of[h, pl.ds(HEAD, 16)].astype(F32)
        return of[h, pl.ds(0, HEAD)].astype(F32), tail[0:1, :] + tail[1:2, :]

    for h in range(2):
        write_state(s1_out, h, own_state[h], own_decay[h])
    for h in range(2):
        lanes = pl.ds(h * HEAD, HEAD)
        cum_col, cum_row = cumulative[h]
        q = silu_float(queries[:, lanes].astype(F32))
        k = silu_float(keys[:, lanes].astype(F32))
        causal = at_t >= at_u
        damping = jnp.where(causal, jnp.exp(jnp.where(causal, cum_col - cum_row, 0.0)), 0.0)
        scores = mm_nt(q, k, highest) * damping
        inside[h] = jnp.dot(scores, values[:, lanes].astype(F32), precision=highest, preferred_element_type=F32)

    count, number = routes_ref.shape[1], router_ref.shape[0]
    expert = lax.broadcasted_iota(jnp.int32, (count, number), 1)
    token = lax.broadcasted_iota(jnp.int32, (count, count), 0)
    after = lax.broadcasted_iota(jnp.int32, (count, count), 1)
    named = [
        jnp.sum(jnp.where(token == after, routes_ref[r : r + 1, :], 0), axis=1, keepdims=True) for r in (0, 1)
    ]
    picks = [(named[r] == expert).astype(F32) for r in (0, 1)]
    earlier = token > after
    taken = mm(earlier.astype(F32).astype(BF16), (picks[0] + picks[1]).astype(BF16))
    slot = lax.broadcasted_iota(jnp.int32, (count, 4 * number), 1)
    hots = []
    for r in (0, 1):
        used = jnp.sum(taken * picks[r], axis=-1, keepdims=True).astype(jnp.int32)
        hots.append((named[r] * 4 + used == slot).astype(F32))
    place = (hots[0] + hots[1]).astype(BF16)

    pl.semaphore_wait(barrier, len(peers))
    state1 = copy(s1_out, s1_in, s1_s, s1_r, twin)
    state1.start()


    def columns(group, d, of_core):
        chip = lax.rem(zh + group, 2) * 4 + lax.rem(y + d, 4)
        return chip * 2 + of_core

    def b_core(group, d):
        src = wo.at[columns(group, d, core)]
        return copy(ow_hbm if (group, d) == (0, 0) else src, src, bc_s.at[group, d], bc_r.at[group, d], twin)

    def b_core_wait(group, d):
        to = wo.at[columns(group, d, 1 - core)]
        copy(to, to, bc_s.at[group, d], bc_r.at[group, d], twin).wait_recv()

    def b_z():
        return copy(ow_hbm, wo.at[columns(0, 0, core)], bz_s, bz_r, at_z(4))

    def b_z_wait():
        to = wo.at[columns(1, 0, core)]
        copy(to, to, bz_s, bz_r, at_z(4)).wait_recv()

    def b_near(group, side):
        src = wo.at[columns(group, 0, core)]
        return copy(
            ow_hbm if group == 0 else src, src, bn_s.at[group, side], bn_r.at[group, side], at_y(3 if side else 1)
        )

    def b_near_wait(group, side):
        to = wo.at[columns(group, 1 if side else 3, core)]
        copy(to, to, bn_s.at[group, side], bn_r.at[group, side], at_y(1)).wait_recv()

    def b_far(group, side):
        to = wo.at[columns(group, 1 if side else 3, core), pl.ds(128 * side, 128)]
        return copy(to, to, bf_s.at[group, side], bf_r.at[group, side], at_y(3 if side else 1))

    def b_far_wait(group, side):
        to = wo.at[columns(group, 2, core), pl.ds(128 * side, 128)]
        copy(to, to, bf_s.at[group, side], bf_r.at[group, side], at_y(1)).wait_recv()

    def b_first(group):
        for side in (0, 1):
            b_near_wait(group, side)
            b_far(group, side).start()
            b_core(group, 1 if side else 3).start()

    def b_second(group):
        b_far_wait(group, 0)
        b_far_wait(group, 1)
        b_core(group, 2).start()

    own_columns = pltpu.make_async_copy(ow_hbm, wo.at[columns(0, 0, core)], load_sem.at[3])
    own_columns.start()
    b_z().start()
    b_core(0, 0).start()

    state1.wait_recv()
    first_core = core == 0
    twin_state = []
    for h in range(2):
        state, decay = read_state(s1_in, h)
        twin_state.append((state, decay))
        chip_state = jnp.where(
            first_core, decay * own_state[h] + state, own_decay[h] * state + own_state[h]
        )
        write_state(s2.at[y], h, chip_state, own_decay[h] * decay)

    def state2(d):
        return copy(s2.at[y], s2.at[y], s2_s.at[d - 1], s2_r.at[d - 1], at_y(d))

    for d in (2, 1, 3):
        state2(d).start()
    b_near(0, 0).start()
    b_near(0, 1).start()
    for c in swaps + own_loads:
        c.start()
    for d in (1, 2, 3):
        source = s2.at[lax.rem(y + 4 - d, 4)]
        copy(source, source, s2_s.at[d - 1], s2_r.at[d - 1], at_y(d)).wait_recv()
    entering = []
    for h in range(2):
        total = jnp.zeros((HEAD, HEAD), F32)
        before = jnp.zeros((HEAD, HEAD), F32)
        factor = jnp.ones((1, HEAD), F32)
        for other in range(4):
            state, decay = read_state(s2.at[other], h)
            before = jnp.where(other == y, total, before)
            factor = jnp.where(other < y, factor * decay, factor)
            total = decay * total + state
        s3_out[h] = total.astype(BF16)
        entering.append((before, factor))
    state3 = copy(s3_out, s3_in, s3_s, s3_r, at_z(4))

    @pl.when(zh == 0)
    def _():
        state3.start()
        s3_in[...] = jnp.zeros_like(s3_in)

    b_first(0)

    b_z_wait()
    b_near(1, 0).start()
    b_near(1, 1).start()
    b_core(1, 0).start()

    @pl.when(zh == 1)
    def _():
        state3.wait_recv()

    for h in range(2):
        lanes = pl.ds(h * HEAD, HEAD)
        before, factor = entering[h]
        state, decay = twin_state[h]
        prefix = factor * s3_in[h].astype(F32) + before
        prefix = jnp.where(first_core, prefix, decay * prefix + state)
        q = silu_float(queries[:, lanes].astype(F32))
        carried = jnp.dot(q, prefix, precision=highest, preferred_element_type=F32)
        heads_out = inside[h] + jnp.exp(cumulative[h][0]) * carried
        mean_square = jnp.mean(heads_out * heads_out, axis=-1, keepdims=True)
        nh[:, lanes] = (heads_out * lax.rsqrt(mean_square + 1e-06) * head_gain[:, lanes]).astype(BF16)
    b_second(0)
    own_columns.wait()
    for d in range(4):
        b_core_wait(0, d)

    def ring_copies(j, buf, size, opp, near, so, ro, sn, rn, at, mine):
        half = size // 2
        far_a = pl.ds(pl.multiple_of(lax.rem(mine + 2, 4) * size, size), half)
        far_b = pl.ds(pl.multiple_of(lax.rem(mine + 2, 4) * size + half, half), half)
        right = rows(lax.rem(mine + 1, 4) * size, size)
        left = rows(lax.rem(mine + 3, 4) * size, size)
        return (
            copy(buf.at[j, far_a], opp.at[j, 0], so.at[j, 0], ro.at[j, 0], at(1)),
            copy(buf.at[j, far_b], opp.at[j, 1], so.at[j, 1], ro.at[j, 1], at(3)),
            copy(buf.at[j, right], near.at[j, 0], sn.at[j, 0], rn.at[j, 0], at(1)),
            copy(buf.at[j, left], near.at[j, 1], sn.at[j, 1], rn.at[j, 1], at(3)),
        )

    def ring_forward(j, buf, size, opp, copies, mine):
        half = size // 2
        copies[0].wait_recv()
        to_right = pl.ds(pl.multiple_of(lax.rem(mine + 1, 4) * size, size), half)
        buf[j, to_right] = (buf[j, to_right].astype(F32) + opp[j, 0].astype(F32)).astype(BF16)
        copies[2].start()
        copies[1].wait_recv()
        to_left = pl.ds(pl.multiple_of(lax.rem(mine + 3, 4) * size + half, half), half)
        buf[j, to_left] = (buf[j, to_left].astype(F32) + opp[j, 1].astype(F32)).astype(BF16)
        copies[3].start()

    def ring_total(j, buf, size, near, copies, mine):
        copies[2].wait_recv()
        copies[3].wait_recv()
        own = rows(mine * size, size)
        return buf[j, own].astype(F32) + near[j, 0].astype(F32) + near[j, 1].astype(F32)

    def c1(j):
        return ring_copies(j, part, 64, c1_opp, c1_nb, c1o_s, c1o_r, c1n_s, c1n_r, at_x, x)

    def c2(j, d):
        to = rows(lax.rem(zl + d, 4) * 16, 16)
        return copy(c2_out.at[j, to], c2_in.at[j, d - 1], c2_s.at[j, d - 1], c2_r.at[j, d - 1], at_line(d))

    def d1(j, d):
        to = rows(lax.rem(x + d, 4) * 16, 16)
        return copy(sent.at[j, to], d1_in.at[j, rows(x * 16, 16)], d1_s.at[j, d - 1], d1_r.at[j, d - 1], at_x(d))

    def d1_wait(j, d):
        source = rows(lax.rem(x + 4 - d, 4) * 16, 16)
        copy(sent.at[j, source], d1_in.at[j, source], d1_s.at[j, d - 1], d1_r.at[j, d - 1], at_x(d)).wait_recv()

    def d2(j, d):
        to = rows(lax.rem(zl + d, 4) * 24, 24)
        return copy(d2_out.at[j, to], d2_in.at[j, rows(z * 24, 24)], d2_s.at[j, d - 1], d2_r.at[j, d - 1], at_z(d))

    def d2_wait(j, d):
        source = rows(lax.rem(z + 8 - d, 8) * 24, 24)
        copy(
            d2_out.at[j, pl.ds(0, 24)], d2_in.at[j, source], d2_s.at[j, d - 1], d2_r.at[j, d - 1], at_z(d)
        ).wait_recv()

    def block(d):
        return rows(lax.rem(y + d, 4) * 48, 48)

    def d3_near(j, side):
        own = block(0)
        return copy(tok.at[j, :, own], tok.at[j, :, own], d3n_s.at[j, side], d3n_r.at[j, side], at_y(3 if side else 1))

    def d3_near_wait(j, side):
        source = block(1 if side else 3)
        copy(tok.at[j, :, source], tok.at[j, :, source], d3n_s.at[j, side], d3n_r.at[j, side], at_y(1)).wait_recv()

    def d3_far(j, side):
        span = block(1 if side else 3)
        return copy(tok.at[j, side, span], tok.at[j, side, span], d3f_s.at[j, side], d3f_r.at[j, side], at_y(3 if side else 1))

    def d3_far_wait(j, side):
        span = block(2)
        copy(tok.at[j, side, span], tok.at[j, side, span], d3f_s.at[j, side], d3f_r.at[j, side], at_y(1)).wait_recv()

    def stage(s, skew, body):
        pl.when((s >= skew) & (s < chunks + skew))(lambda: body(s - skew))

    def number_of(j, group):
        return lax.rem(j + group * (chunks // 2), chunks)

    def project(j):
        @pl.when(j == 2)
        def _():
            b_first(1)

        @pl.when(j == 3)
        def _():
            b_second(1)

        @pl.when(j == chunks // 2)
        def _():
            for d in range(4):
                b_core_wait(1, d)

        for half in (0, 1):
            part[j, :, pl.ds(half * HW, HW)] = mm(nh[...], wo[number_of(j, zh) * 2 + half]).astype(BF16)
        copies = c1(j)
        copies[0].start()
        copies[1].start()

    def project_line(j):
        c2_out[j] = ring_total(j, part, 64, c1_nb, c1(j), x).astype(BF16)
        for d in (3, 2, 1):
            c2(j, d).start()

    def dispatch(j):
        number = number_of(j, zh)
        span = rows(number * CW, CW)
        total = c2_out[j, rows(zl * 16, 16)].astype(F32)
        for d in (1, 2, 3):
            c2(j, d).wait_recv()
            total = total + c2_in[j, d - 1].astype(F32)
        state = res_ref[:, span].astype(F32) + total
        gained = (state * gain_ref[:, span]).astype(BF16)
        sent[j] = mm_tn(place, gained).astype(BF16)
        for d in (2, 1, 3):
            d1(j, d).start()
        d1_in[j, rows(x * 16, 16)] = sent[j, rows(x * 16, 16)]
        hid[number] = state
        ssq[...] += jnp.sum(state * state, axis=-1, keepdims=True)
        logits[...] += mm_nt(gained, router_ref[:, span])

    def dispatch_z(j):
        for d in (1, 2, 3):
            d1_wait(j, d)
        d2_out[j] = (mm(q_ref[0], d1_in[j, :, pl.ds(0, HW)]) + mm(q_ref[1], d1_in[j, :, pl.ds(HW, HW)])).astype(BF16)
        for d in (4, 3, 5, 2, 6, 1, 7):
            d2(j, d).start()
        d2_in[j, rows(z * 24, 24)] = d2_out[j, rows(zl * 24, 24)]

    def gather_near(j):
        for d in range(1, 8):
            d2_wait(j, d)
        arrived = d2_in[j]
        for half in (0, 1):
            packed = mm(pack_ref[half], arrived).astype(BF16)
            for group in (0, 1):
                tok[j, group, block(0), pl.ds(half * HW, HW)] = packed[group * 48 : group * 48 + 48]
        d3_near(j, 0).start()
        d3_near(j, 1).start()

    def gather_far(j):
        for side in (0, 1):
            d3_near_wait(j, side)
            d3_far(j, side).start()

    def multiply(j):
        for side in (0, 1):
            d3_far_wait(j, side)

        @pl.when(j == 0)
        def _():
            swaps[0].wait_recv()
            swaps[1].wait_recv()

        for group in (0, 1):
            span = rows(number_of(j, group) * CW, CW)
            taken = pl.ds(group * 192, 192)
            tokens = tok[j, group]
            for i in range(2):
                acc[i, 0, taken] += mm_nt(tokens, wg[i, :, span])
                acc[i, 1, taken] += mm_nt(tokens, wu[i, :, span])
            plain = tokens.astype(F32) * (1.0 / gain_ref[:, span])
            square = plain * plain
            rowsq[taken] += sum(square[:, k * 128 : (k + 1) * 128] for k in range(CW // 128))

    def cd_step(s, _):
        stage(s, 0, project)
        stage(s, 1, lambda j: ring_forward(j, part, 64, c1_opp, c1(j), x))
        stage(s, 2, project_line)
        stage(s, 3, dispatch)
        stage(s, 4, dispatch_z)
        stage(s, 5, gather_near)
        stage(s, 6, gather_far)
        stage(s, 8, multiply)
        return 0

    for c in own_loads:
        c.wait()
    lax.fori_loop(0, chunks + 8, cd_step, 0)
    swaps[2].wait_recv()
    per_width = 1.0 / (chunks * CW)
    scale = lax.rsqrt(jnp.sum(rowsq[...], axis=-1, keepdims=True) * per_width + 1e-06)
    for i in range(2):
        gate = acc[i, 0] * scale
        act[i] = (gate * jax.nn.sigmoid(gate) * (acc[i, 1] * scale)).astype(BF16)

    @pl.loop(0, chunks)
    def _(j):
        for side in (0, 1):
            d3_near(j, side).wait_send()
            d3_far(j, side).wait_send()

    router_out = logits[...] * lax.rsqrt(ssq[:, 0:1] * per_width + 1e-06)
    picked0 = jnp.sum(router_out * picks[0], axis=-1, keepdims=True)
    picked1 = jnp.sum(router_out * picks[1], axis=-1, keepdims=True)
    mix = jax.nn.sigmoid(picked0 - picked1) * hots[0] + jax.nn.sigmoid(picked1 - picked0) * hots[1]
    mix_hi = mix.astype(BF16)
    mix_lo = (mix - mix_hi.astype(F32)).astype(BF16)

    def f1(j):
        return (
            copy(tok.at[j, 0, block(2)], f_opp.at[j, 0], fo_s.at[j, 0], fo_r.at[j, 0], at_y(1)),
            copy(tok.at[j, 1, block(2)], f_opp.at[j, 1], fo_s.at[j, 1], fo_r.at[j, 1], at_y(3)),
            copy(tok.at[j, :, block(1)], f_nb.at[j, 0], fn_s.at[j, 0], fn_r.at[j, 0], at_y(1)),
            copy(tok.at[j, :, block(3)], f_nb.at[j, 1], fn_s.at[j, 1], fn_r.at[j, 1], at_y(3)),
        )

    def sum_far(j):
        copies = f1(j)
        for side in (0, 1):
            copies[side].wait_recv()
            span = block(3 if side else 1)
            tok[j, side, span] = (tok[j, side, span].astype(F32) + f_opp[j, side].astype(F32)).astype(BF16)
            copies[2 + side].start()

    def sum_near(j):
        copies = f1(j)
        copies[2].wait_recv()
        copies[3].wait_recv()
        total = tok[j, :, block(0)].astype(F32) + f_nb[j, 0].astype(F32) + f_nb[j, 1].astype(F32)
        return total.astype(BF16).reshape(96, CW)

    def g2(j, d):
        to = rows(lax.rem(z + d, 8) * 24, 24)
        return copy(g2_out.at[j, to], g2_in.at[j, rows(z * 24, 24)], g2_s.at[j, d - 1], g2_r.at[j, d - 1], at_z(d))

    def g2_wait(j, d):
        source = rows(lax.rem(z + 8 - d, 8) * 24, 24)
        copy(
            g2_out.at[j, source], g2_in.at[j, source], g2_s.at[j, d - 1], g2_r.at[j, d - 1], at_z(d)
        ).wait_recv()

    def g3(j, d):
        to = rows(lax.rem(x + d, 4) * 16, 16)
        return copy(g3_out.at[j, to], g3_in.at[j, rows(x * 16, 16)], g3_s.at[j, d - 1], g3_r.at[j, d - 1], at_x(d))

    def g3_wait(j, d):
        source = rows(lax.rem(x + 4 - d, 4) * 16, 16)
        copy(
            g3_out.at[j, source], g3_in.at[j, source], g3_s.at[j, d - 1], g3_r.at[j, d - 1], at_x(d)
        ).wait_recv()

    def down(j):
        span = rows(j * CW, CW)
        both = (mm(act[0], wd[0, :, span]) + mm(act[1], wd[1, :, span])).astype(BF16)
        tok[j] = both.reshape(2, 192, CW)
        copies = f1(j)
        copies[0].start()
        copies[1].start()

    def return_z(j):
        total = sum_near(j)
        g2_out[j] = (mm(unpack_ref[0], total[:, :HW]) + mm(unpack_ref[1], total[:, HW:])).astype(BF16)
        for d in (4, 3, 5, 2, 6, 1, 7):
            g2(j, d).start()
        g2_in[j, rows(z * 24, 24)] = g2_out[j, rows(z * 24, 24)]

    def return_x(j):
        for d in range(1, 8):
            g2_wait(j, d)
        total = (g2_in[j, pl.ds(0, 96)].astype(F32) + g2_in[j, pl.ds(96, 96)].astype(F32)).astype(BF16)
        g3_out[j, :, pl.ds(0, HW)] = mm(qt_ref[0], total).astype(BF16)
        g3_out[j, :, pl.ds(HW, HW)] = mm(qt_ref[1], total).astype(BF16)
        for d in (2, 1, 3):
            g3(j, d).start()
        g3_in[j, rows(x * 16, 16)] = g3_out[j, rows(x * 16, 16)]

    def combine(j):
        for d in (1, 2, 3):
            g3_wait(j, d)
        back = g3_in[j]
        out_ref[:, rows(j * CW, CW)] = (hid[j] + mm(mix_hi, back) + mm(mix_lo, back)).astype(BF16)

    def f_step(s, _):
        stage(s, 0, down)
        stage(s, 1, sum_far)
        stage(s, 2, return_z)
        stage(s, 3, return_x)
        stage(s, 4, combine)
        return 0

    lax.fori_loop(0, chunks + 4, f_step, 0)

    @pl.loop(0, chunks)
    def _(j):
        for c in c1(j) + f1(j):
            c.wait_send()
        for d in (1, 2, 3):
            c2(j, d).wait_send()
            d1(j, d).wait_send()
            g3(j, d).wait_send()
        for d in range(1, 8):
            d2(j, d).wait_send()
            g2(j, d).wait_send()
    for c in swaps + [state1, b_z()] + [state2(d) for d in (1, 2, 3)]:
        c.wait_send()
    for group in range(2):
        for side in range(2):
            b_near(group, side).wait_send()
            b_far(group, side).wait_send()
        for d in range(4):
            b_core(group, d).wait_send()

    @pl.when(zh == 0)
    def _():
        state3.wait_send()


def selections():
    q = np.zeros((2, 96, 64), np.float32)
    pack = np.zeros((2, 96, 192), np.float32)
    for half in range(2):
        for e in range(4):
            for source in range(4):
                for s in range(3):
                    q[half, e * 24 + half * 12 + source * 3 + s, source * 16 + e * 4 + s] = 1
        for source in range(8):
            for r in range(12):
                pack[half, source * 12 + r, source * 24 + half * 12 + r] = 1
    return tuple(jnp.asarray(a, BF16) for a in (q, q.transpose(0, 2, 1), pack, pack.transpose(0, 2, 1)))


def shards(
    queries,
    keys_in,
    values_in,
    log_decay,
    attn_gain,
    out_weight,
    residual,
    moe_gain,
    router,
    gate_weight,
    up_weight,
    down_weight,
    routes,
):
    length, _, span = queries.shape
    count, _, width = residual.shape
    hidden = gate_weight.shape[2]
    n = width // CW
    flat = lambda a: a.reshape(length, span)
    dma = lambda *shape: pltpu.SemaphoreType.DMA(shape)
    vmem = lambda *shape: pltpu.VMEM(shape, BF16)
    scratch = [
        vmem(length, span), vmem(2 * n, span, HW), pltpu.VMEM((2, length, HEAD), F32),
        vmem(2, 144, HEAD), vmem(2, 144, HEAD), vmem(4, 2, 144, HEAD), vmem(2, HEAD, HEAD), vmem(2, HEAD, HEAD),
        vmem(2, hidden, width), vmem(2, hidden, width), vmem(2, hidden, width),
        vmem(n, 256, CW), vmem(n, 2, 32, CW), vmem(n, 2, 64, CW), vmem(n, 64, CW), vmem(n, 3, 16, CW),
        pltpu.VMEM((n, 16, CW), F32), pltpu.VMEM((16, 128), F32), pltpu.VMEM((384, 128), F32),
        vmem(n, 64, CW), vmem(n, 64, CW), vmem(n, 96, HW), vmem(n, 192, HW), vmem(n, 2, 192, CW),
        pltpu.VMEM((16, 16), F32), pltpu.VMEM((2, 2, 384, hidden), F32), vmem(2, 384, hidden),
        vmem(n, 2, 48, CW), vmem(n, 2, 2, 48, CW), vmem(n, 192, HW), vmem(n, 192, HW), vmem(n, 64, CW), vmem(n, 64, CW),
        dma(4), dma(3), dma(3), pltpu.SemaphoreType.DMA, pltpu.SemaphoreType.DMA, dma(3), dma(3),
        pltpu.SemaphoreType.DMA, pltpu.SemaphoreType.DMA,
        dma(2, 4), dma(2, 4), pltpu.SemaphoreType.DMA, pltpu.SemaphoreType.DMA, dma(2, 2), dma(2, 2), dma(2, 2), dma(2, 2),
    ]
    for lanes in (2, 2, 3, 3, 7, 2, 2, 2, 2, 7, 3):
        scratch += [dma(n, lanes), dma(n, lanes)]
    in_vmem = pl.BlockSpec(memory_space=pltpu.VMEM)
    in_hbm = pl.BlockSpec(memory_space=pl.ANY)
    mixed = pl.pallas_call(
        block_kernel,
        out_shape=jax.ShapeDtypeStruct((count, width), BF16),
        in_specs=[in_vmem] * 5 + [in_hbm] + [in_vmem] * 8 + [in_hbm] * 3,
        out_specs=in_vmem,
        scratch_shapes=scratch,
        compiler_params=pltpu.CompilerParams(collective_id=0, has_side_effects=True, vmem_limit_bytes=67043328),
    )(
        flat(queries), flat(keys_in), flat(values_in), log_decay, attn_gain.reshape(1, span),
        out_weight, residual.reshape(count, width), moe_gain.reshape(1, width), router.T, routes.reshape(count, 2).T,
        *selections(), jnp.swapaxes(gate_weight, 1, 2), jnp.swapaxes(up_weight, 1, 2), down_weight,
    )
    return mixed.reshape(residual.shape)


def solution(mesh):
    return jax.shard_map(
        shards,
        mesh=mesh,
        in_specs=(
            P("ctx", None, "ep"),
            P("ctx", None, "ep"),
            P("ctx", None, "ep"),
            P("ep", None, "ctx"),
            P("ep"),
            P("ep", "ctx"),
            P(("ctx", "ep"), None, None),
            P(),
            P(),
            P("ep", None, "ctx"),
            P("ep", None, "ctx"),
            P("ep", "ctx", None),
            P(("ctx", "ep"), None, None),
        ),
        out_specs=P(("ctx", "ep"), None, None),
        check_vma=False,
    )
```

```python
import jax
import jax.numpy as jnp
import numpy as np
from jax import lax
from jax.experimental import pallas as pl
from jax.experimental.pallas import tpu as pltpu
from jax.sharding import PartitionSpec as P

MESH = pl.DeviceIdType.MESH
F32, BF16 = jnp.float32, jnp.bfloat16
CW = 768
HW = CW // 2
CF = 512
HF = CF // 2
HEAD = 128


def silu_float(values):
    return values * jax.nn.sigmoid(values)


def place_of():
    ctx, ep = lax.axis_index("ctx"), lax.axis_index("ep")
    y, core = lax.rem(ctx, 8) // 2, lax.rem(ctx, 2)
    z = (ctx // 8) * 4 + lax.rem(ep, 4)
    return ep // 4, y, z, core


def device_at(x, y, z, core):
    return ((z // 4) * 8 + y * 2 + core, x * 4 + lax.rem(z, 4))


def mm(a, b):
    return jnp.dot(a, b, preferred_element_type=F32)


def mm_nt(a, b, precision=None):
    return lax.dot_general(a, b, (((1,), (1,)), ((), ())), precision=precision, preferred_element_type=F32)


def mm_tn(a, b, precision=None):
    return lax.dot_general(a, b, (((0,), (0,)), ((), ())), precision=precision, preferred_element_type=F32)


def rows(start, size):
    return pl.ds(pl.multiple_of(start, size), size)


def block_kernel(
    queries, keys, values, decay_ref, head_gain, ow_hbm, res_ref, gain_ref, router_ref, routes_ref,
    q_ref, qt_ref, pack_ref, unpack_ref, gate_hbm, up_hbm, down_hbm,
    out_ref,
    nh, wo, inside, s1_out, s1_in, s2, s3_out, s3_in,
    wg, wu, wd, part, c1_opp, c1_nb, c2_out, c2_in, hid, ssq, rowsq, sent, d1_in, d2_out, d2_in, tok, logits,
    acc, act, down_out, f_opp, f_nb, g2_out, g2_in, g3_out, g3_in,
    load_sem, swap_s, swap_r, s1_s, s1_r, s2_s, s2_r, s3_s, s3_r,
    bc_s, bc_r, bz_s, bz_r, bn_s, bn_r, bf_s, bf_r,
    c1o_s, c1o_r, c1n_s, c1n_r, c2_s, c2_r, d1_s, d1_r, d2_s, d2_r, d3n_s, d3n_r, d3f_s, d3f_r,
    fo_s, fo_r, fn_s, fn_r, g2_s, g2_r, g3_s, g3_r,
):
    x, y, z, core = place_of()
    zl, zh = lax.rem(z, 4), z // 4
    chunks = hid.shape[1] // CW
    back_chunks = hid.shape[1] // CF

    def at_x(d):
        return device_at(lax.rem(x + d, 4), y, z, core)

    def at_y(d):
        return device_at(x, lax.rem(y + d, 4), z, core)

    def at_z(d):
        return device_at(x, y, lax.rem(z + d, 8), core)

    def at_line(d):
        return device_at(x, y, zh * 4 + lax.rem(zl + d, 4), core)

    def copy(src, dst, send, recv, to):
        return pltpu.make_async_remote_copy(
            src_ref=src, dst_ref=dst, send_sem=send, recv_sem=recv, device_id=to, device_id_type=MESH
        )

    twin = device_at(x, y, z, 1 - core)
    barrier = pltpu.get_barrier_semaphore()
    peers = [twin] + [at_x(d) for d in (1, 2, 3)] + [at_y(d) for d in (1, 2, 3)] + [at_z(d) for d in range(1, 8)]
    for peer in peers:
        pl.semaphore_signal(barrier, inc=1, device_id=peer, device_id_type=MESH)
    weights = ((gate_hbm.at[0], wg), (up_hbm.at[0], wu), (down_hbm.at[0], wd))
    own_loads = [pltpu.make_async_copy(w, to.at[0], load_sem.at[i]) for i, (w, to) in enumerate(weights)]
    swaps = [copy(w, to.at[1], swap_s.at[i], swap_r.at[i], twin) for i, (w, to) in enumerate(weights)]
    ssq[...] = jnp.zeros_like(ssq)
    rowsq[...] = jnp.zeros_like(rowsq)
    logits[...] = jnp.zeros_like(logits)
    acc[...] = jnp.zeros_like(acc)

    length = queries.shape[0]
    at_t = lax.broadcasted_iota(jnp.int32, (length, length), 0)
    at_u = lax.broadcasted_iota(jnp.int32, (length, length), 1)
    highest = lax.Precision.HIGHEST
    own_state, own_decay, cumulative = [], [], []
    for h in range(2):
        lanes = pl.ds(h * HEAD, HEAD)
        log_row = decay_ref[h]
        log_col = jnp.sum(jnp.where(at_u == at_t, log_row, 0.0), axis=1, keepdims=True)
        cum_col = jnp.sum(jnp.where(at_u <= at_t, log_row, 0.0), axis=1, keepdims=True)
        cum_row = jnp.sum(jnp.where(at_t <= at_u, log_col, 0.0), axis=0, keepdims=True)
        last = jnp.sum(log_row, axis=1, keepdims=True)
        k = silu_float(keys[:, lanes].astype(F32))
        own_state.append(mm_tn(k * jnp.exp(last - cum_col), values[:, lanes].astype(F32), highest))
        own_decay.append(jnp.broadcast_to(jnp.exp(last), (1, HEAD)))
        cumulative.append((cum_col, cum_row))

    def write_state(to, h, state, decay):
        high = decay.astype(BF16)
        low = (decay - high.astype(F32)).astype(BF16)
        first = lax.broadcasted_iota(jnp.int32, (16, HEAD), 0) == 0
        to[h, pl.ds(0, HEAD)] = state.astype(BF16)
        to[h, pl.ds(HEAD, 16)] = jnp.where(first, high.astype(F32), low.astype(F32)).astype(BF16)

    def read_state(of, h):
        tail = of[h, pl.ds(HEAD, 16)].astype(F32)
        return of[h, pl.ds(0, HEAD)].astype(F32), tail[0:1, :] + tail[1:2, :]

    for h in range(2):
        write_state(s1_out, h, own_state[h], own_decay[h])
    for h in range(2):
        lanes = pl.ds(h * HEAD, HEAD)
        cum_col, cum_row = cumulative[h]
        q = silu_float(queries[:, lanes].astype(F32))
        k = silu_float(keys[:, lanes].astype(F32))
        causal = at_t >= at_u
        damping = jnp.where(causal, jnp.exp(jnp.where(causal, cum_col - cum_row, 0.0)), 0.0)
        scores = mm_nt(q, k, highest) * damping
        inside[h] = jnp.dot(scores, values[:, lanes].astype(F32), precision=highest, preferred_element_type=F32)

    count, number = routes_ref.shape[1], router_ref.shape[0]
    expert = lax.broadcasted_iota(jnp.int32, (count, number), 1)
    token = lax.broadcasted_iota(jnp.int32, (count, count), 0)
    after = lax.broadcasted_iota(jnp.int32, (count, count), 1)
    named = [
        jnp.sum(jnp.where(token == after, routes_ref[r : r + 1, :], 0), axis=1, keepdims=True) for r in (0, 1)
    ]
    picks = [(named[r] == expert).astype(F32) for r in (0, 1)]
    earlier = token > after
    taken = mm(earlier.astype(F32).astype(BF16), (picks[0] + picks[1]).astype(BF16))
    slot = lax.broadcasted_iota(jnp.int32, (count, 4 * number), 1)
    hots = []
    for r in (0, 1):
        used = jnp.sum(taken * picks[r], axis=-1, keepdims=True).astype(jnp.int32)
        hots.append((named[r] * 4 + used == slot).astype(F32))
    place = (hots[0] + hots[1]).astype(BF16)

    pl.semaphore_wait(barrier, len(peers))
    state1 = copy(s1_out, s1_in, s1_s, s1_r, twin)
    state1.start()


    def columns(group, d, of_core):
        chip = lax.rem(zh + group, 2) * 4 + lax.rem(y + d, 4)
        return chip * 2 + of_core

    def b_core(group, d):
        src = wo.at[columns(group, d, core)]
        return copy(ow_hbm if (group, d) == (0, 0) else src, src, bc_s.at[group, d], bc_r.at[group, d], twin)

    def b_core_wait(group, d):
        to = wo.at[columns(group, d, 1 - core)]
        copy(to, to, bc_s.at[group, d], bc_r.at[group, d], twin).wait_recv()

    def b_z():
        return copy(ow_hbm, wo.at[columns(0, 0, core)], bz_s, bz_r, at_z(4))

    def b_z_wait():
        to = wo.at[columns(1, 0, core)]
        copy(to, to, bz_s, bz_r, at_z(4)).wait_recv()

    def b_near(group, side):
        src = wo.at[columns(group, 0, core)]
        return copy(
            ow_hbm if group == 0 else src, src, bn_s.at[group, side], bn_r.at[group, side], at_y(3 if side else 1)
        )

    def b_near_wait(group, side):
        to = wo.at[columns(group, 1 if side else 3, core)]
        copy(to, to, bn_s.at[group, side], bn_r.at[group, side], at_y(1)).wait_recv()

    def b_far(group, side):
        to = wo.at[columns(group, 1 if side else 3, core), pl.ds(128 * side, 128)]
        return copy(to, to, bf_s.at[group, side], bf_r.at[group, side], at_y(3 if side else 1))

    def b_far_wait(group, side):
        to = wo.at[columns(group, 2, core), pl.ds(128 * side, 128)]
        copy(to, to, bf_s.at[group, side], bf_r.at[group, side], at_y(1)).wait_recv()

    def b_first(group):
        for side in (0, 1):
            b_near_wait(group, side)
            b_far(group, side).start()
            b_core(group, 1 if side else 3).start()

    def b_second(group):
        b_far_wait(group, 0)
        b_far_wait(group, 1)
        b_core(group, 2).start()

    own_columns = pltpu.make_async_copy(ow_hbm, wo.at[columns(0, 0, core)], load_sem.at[3])
    own_columns.start()
    b_z().start()
    b_core(0, 0).start()

    state1.wait_recv()
    first_core = core == 0
    twin_state = []
    for h in range(2):
        state, decay = read_state(s1_in, h)
        twin_state.append((state, decay))
        chip_state = jnp.where(
            first_core, decay * own_state[h] + state, own_decay[h] * state + own_state[h]
        )
        write_state(s2.at[y], h, chip_state, own_decay[h] * decay)

    def state2(d):
        return copy(s2.at[y], s2.at[y], s2_s.at[d - 1], s2_r.at[d - 1], at_y(d))

    for d in (2, 1, 3):
        state2(d).start()
    b_near(0, 0).start()
    b_near(0, 1).start()
    for c in swaps + own_loads:
        c.start()
    for d in (1, 2, 3):
        source = s2.at[lax.rem(y + 4 - d, 4)]
        copy(source, source, s2_s.at[d - 1], s2_r.at[d - 1], at_y(d)).wait_recv()
    entering = []
    for h in range(2):
        total = jnp.zeros((HEAD, HEAD), F32)
        before = jnp.zeros((HEAD, HEAD), F32)
        factor = jnp.ones((1, HEAD), F32)
        for other in range(4):
            state, decay = read_state(s2.at[other], h)
            before = jnp.where(other == y, total, before)
            factor = jnp.where(other < y, factor * decay, factor)
            total = decay * total + state
        s3_out[h] = total.astype(BF16)
        entering.append((before, factor))
    state3 = copy(s3_out, s3_in, s3_s, s3_r, at_z(4))

    @pl.when(zh == 0)
    def _():
        state3.start()
        s3_in[...] = jnp.zeros_like(s3_in)

    b_first(0)

    b_z_wait()
    b_near(1, 0).start()
    b_near(1, 1).start()
    b_core(1, 0).start()

    @pl.when(zh == 1)
    def _():
        state3.wait_recv()

    for h in range(2):
        lanes = pl.ds(h * HEAD, HEAD)
        before, factor = entering[h]
        state, decay = twin_state[h]
        prefix = factor * s3_in[h].astype(F32) + before
        prefix = jnp.where(first_core, prefix, decay * prefix + state)
        q = silu_float(queries[:, lanes].astype(F32))
        carried = jnp.dot(q, prefix, precision=highest, preferred_element_type=F32)
        heads_out = inside[h] + jnp.exp(cumulative[h][0]) * carried
        mean_square = jnp.mean(heads_out * heads_out, axis=-1, keepdims=True)
        nh[:, lanes] = (heads_out * lax.rsqrt(mean_square + 1e-06) * head_gain[:, lanes]).astype(BF16)
    b_second(0)
    own_columns.wait()
    for d in range(4):
        b_core_wait(0, d)

    def ring_copies(j, buf, size, opp, near, so, ro, sn, rn, at, mine):
        half = size // 2
        far_a = pl.ds(pl.multiple_of(lax.rem(mine + 2, 4) * size, size), half)
        far_b = pl.ds(pl.multiple_of(lax.rem(mine + 2, 4) * size + half, half), half)
        right = rows(lax.rem(mine + 1, 4) * size, size)
        left = rows(lax.rem(mine + 3, 4) * size, size)
        return (
            copy(buf.at[j, far_a], opp.at[j, 0], so.at[j, 0], ro.at[j, 0], at(1)),
            copy(buf.at[j, far_b], opp.at[j, 1], so.at[j, 1], ro.at[j, 1], at(3)),
            copy(buf.at[j, right], near.at[j, 0], sn.at[j, 0], rn.at[j, 0], at(1)),
            copy(buf.at[j, left], near.at[j, 1], sn.at[j, 1], rn.at[j, 1], at(3)),
        )

    def ring_forward(j, buf, size, opp, copies, mine):
        half = size // 2
        copies[0].wait_recv()
        to_right = pl.ds(pl.multiple_of(lax.rem(mine + 1, 4) * size, size), half)
        buf[j, to_right] = (buf[j, to_right].astype(F32) + opp[j, 0].astype(F32)).astype(BF16)
        copies[2].start()
        copies[1].wait_recv()
        to_left = pl.ds(pl.multiple_of(lax.rem(mine + 3, 4) * size + half, half), half)
        buf[j, to_left] = (buf[j, to_left].astype(F32) + opp[j, 1].astype(F32)).astype(BF16)
        copies[3].start()

    def ring_total(j, buf, size, near, copies, mine):
        copies[2].wait_recv()
        copies[3].wait_recv()
        own = rows(mine * size, size)
        return buf[j, own].astype(F32) + near[j, 0].astype(F32) + near[j, 1].astype(F32)

    def c1(j):
        return ring_copies(j, part, 64, c1_opp, c1_nb, c1o_s, c1o_r, c1n_s, c1n_r, at_x, x)

    def c2(j, d):
        to = rows(lax.rem(zl + d, 4) * 16, 16)
        return copy(c2_out.at[j, to], c2_in.at[j, d - 1], c2_s.at[j, d - 1], c2_r.at[j, d - 1], at_line(d))

    def d1(j, d):
        to = rows(lax.rem(x + d, 4) * 16, 16)
        return copy(sent.at[j, to], d1_in.at[j, rows(x * 16, 16)], d1_s.at[j, d - 1], d1_r.at[j, d - 1], at_x(d))

    def d1_wait(j, d):
        source = rows(lax.rem(x + 4 - d, 4) * 16, 16)
        copy(sent.at[j, source], d1_in.at[j, source], d1_s.at[j, d - 1], d1_r.at[j, d - 1], at_x(d)).wait_recv()

    def d2(j, d):
        to = rows(lax.rem(zl + d, 4) * 24, 24)
        return copy(d2_out.at[j, to], d2_in.at[j, rows(z * 24, 24)], d2_s.at[j, d - 1], d2_r.at[j, d - 1], at_z(d))

    def d2_wait(j, d):
        source = rows(lax.rem(z + 8 - d, 8) * 24, 24)
        copy(
            d2_out.at[j, pl.ds(0, 24)], d2_in.at[j, source], d2_s.at[j, d - 1], d2_r.at[j, d - 1], at_z(d)
        ).wait_recv()

    def block(d):
        return rows(lax.rem(y + d, 4) * 48, 48)

    def d3_near(j, side):
        own = block(0)
        return copy(tok.at[j, :, own], tok.at[j, :, own], d3n_s.at[j, side], d3n_r.at[j, side], at_y(3 if side else 1))

    def d3_near_wait(j, side):
        source = block(1 if side else 3)
        copy(tok.at[j, :, source], tok.at[j, :, source], d3n_s.at[j, side], d3n_r.at[j, side], at_y(1)).wait_recv()

    def d3_far(j, side):
        span = block(1 if side else 3)
        return copy(tok.at[j, side, span], tok.at[j, side, span], d3f_s.at[j, side], d3f_r.at[j, side], at_y(3 if side else 1))

    def d3_far_wait(j, side):
        span = block(2)
        copy(tok.at[j, side, span], tok.at[j, side, span], d3f_s.at[j, side], d3f_r.at[j, side], at_y(1)).wait_recv()

    def stage(s, skew, body):
        pl.when((s >= skew) & (s < chunks + skew))(lambda: body(s - skew))

    def number_of(j, group):
        return lax.rem(j + group * (chunks // 2), chunks)

    def project(j):
        @pl.when(j == 2)
        def _():
            b_first(1)

        @pl.when(j == 3)
        def _():
            b_second(1)

        @pl.when(j == chunks // 2)
        def _():
            for d in range(4):
                b_core_wait(1, d)

        for half in (0, 1):
            part[j, :, pl.ds(half * HW, HW)] = mm(nh[...], wo[number_of(j, zh) * 2 + half]).astype(BF16)
        copies = c1(j)
        copies[0].start()
        copies[1].start()

    def project_line(j):
        c2_out[j] = ring_total(j, part, 64, c1_nb, c1(j), x).astype(BF16)
        for d in (3, 2, 1):
            c2(j, d).start()

    def dispatch(j):
        number = number_of(j, zh)
        span = rows(number * CW, CW)
        total = c2_out[j, rows(zl * 16, 16)].astype(F32)
        for d in (1, 2, 3):
            c2(j, d).wait_recv()
            total = total + c2_in[j, d - 1].astype(F32)
        state = res_ref[:, span].astype(F32) + total
        gained = (state * gain_ref[:, span]).astype(BF16)
        sent[j] = mm_tn(place, gained).astype(BF16)
        for d in (2, 1, 3):
            d1(j, d).start()
        d1_in[j, rows(x * 16, 16)] = sent[j, rows(x * 16, 16)]
        hid[:, span] = state
        ssq[...] += jnp.sum(state * state, axis=-1, keepdims=True)
        logits[...] += mm_nt(gained, router_ref[:, span])

    def dispatch_z(j):
        for d in (1, 2, 3):
            d1_wait(j, d)
        d2_out[j] = (mm(q_ref[0], d1_in[j, :, pl.ds(0, HW)]) + mm(q_ref[1], d1_in[j, :, pl.ds(HW, HW)])).astype(BF16)
        for d in (4, 3, 5, 2, 6, 1, 7):
            d2(j, d).start()
        d2_in[j, rows(z * 24, 24)] = d2_out[j, rows(zl * 24, 24)]

    def gather_near(j):
        for d in range(1, 8):
            d2_wait(j, d)
        arrived = d2_in[j]
        for half in (0, 1):
            packed = mm(pack_ref[half], arrived).astype(BF16)
            for group in (0, 1):
                tok[j, group, block(0), pl.ds(half * HW, HW)] = packed[group * 48 : group * 48 + 48]
        d3_near(j, 0).start()
        d3_near(j, 1).start()

    def gather_far(j):
        for side in (0, 1):
            d3_near_wait(j, side)
            d3_far(j, side).start()

    def multiply(j):
        for side in (0, 1):
            d3_far_wait(j, side)

        @pl.when(j == 0)
        def _():
            swaps[0].wait_recv()
            swaps[1].wait_recv()

        for group in (0, 1):
            span = rows(number_of(j, group) * CW, CW)
            taken = pl.ds(group * 192, 192)
            tokens = tok[j, group]
            for i in range(2):
                acc[i, 0, taken] += mm_nt(tokens, wg[i, :, span])
                acc[i, 1, taken] += mm_nt(tokens, wu[i, :, span])
            plain = tokens.astype(F32) * (1.0 / gain_ref[:, span])
            square = plain * plain
            rowsq[taken] += sum(square[:, k * 128 : (k + 1) * 128] for k in range(CW // 128))

    def cd_step(s, _):
        stage(s, 0, project)
        stage(s, 1, lambda j: ring_forward(j, part, 64, c1_opp, c1(j), x))
        stage(s, 2, project_line)
        stage(s, 3, dispatch)
        stage(s, 4, dispatch_z)
        stage(s, 5, gather_near)
        stage(s, 6, gather_far)
        stage(s, 8, multiply)
        return 0

    for c in own_loads:
        c.wait()
    lax.fori_loop(0, chunks + 8, cd_step, 0)
    swaps[2].wait_recv()
    per_width = 1.0 / (chunks * CW)
    scale = lax.rsqrt(jnp.sum(rowsq[...], axis=-1, keepdims=True) * per_width + 1e-06)
    for i in range(2):
        gate = acc[i, 0] * scale
        act[i] = (gate * jax.nn.sigmoid(gate) * (acc[i, 1] * scale)).astype(BF16)

    @pl.loop(0, chunks)
    def _(j):
        for side in (0, 1):
            d3_near(j, side).wait_send()
            d3_far(j, side).wait_send()

    router_out = logits[...] * lax.rsqrt(ssq[:, 0:1] * per_width + 1e-06)
    picked0 = jnp.sum(router_out * picks[0], axis=-1, keepdims=True)
    picked1 = jnp.sum(router_out * picks[1], axis=-1, keepdims=True)
    mix = jax.nn.sigmoid(picked0 - picked1) * hots[0] + jax.nn.sigmoid(picked1 - picked0) * hots[1]
    mix_hi = mix.astype(BF16)
    mix_lo = (mix - mix_hi.astype(F32)).astype(BF16)

    def f1(j):
        return (
            copy(down_out.at[j, 0, block(2)], f_opp.at[j, 0], fo_s.at[j, 0], fo_r.at[j, 0], at_y(1)),
            copy(down_out.at[j, 1, block(2)], f_opp.at[j, 1], fo_s.at[j, 1], fo_r.at[j, 1], at_y(3)),
            copy(down_out.at[j, :, block(1)], f_nb.at[j, 0], fn_s.at[j, 0], fn_r.at[j, 0], at_y(1)),
            copy(down_out.at[j, :, block(3)], f_nb.at[j, 1], fn_s.at[j, 1], fn_r.at[j, 1], at_y(3)),
        )

    def sum_far(j):
        copies = f1(j)
        for side in (0, 1):
            copies[side].wait_recv()
            span = block(3 if side else 1)
            down_out[j, side, span] = (down_out[j, side, span].astype(F32) + f_opp[j, side].astype(F32)).astype(BF16)
            copies[2 + side].start()

    def sum_near(j):
        copies = f1(j)
        copies[2].wait_recv()
        copies[3].wait_recv()
        total = down_out[j, :, block(0)].astype(F32) + f_nb[j, 0].astype(F32) + f_nb[j, 1].astype(F32)
        return total.astype(BF16).reshape(96, CF)

    def g2(j, d):
        to = rows(lax.rem(z + d, 8) * 24, 24)
        return copy(g2_out.at[j, to], g2_in.at[j, rows(z * 24, 24)], g2_s.at[j, d - 1], g2_r.at[j, d - 1], at_z(d))

    def g2_wait(j, d):
        source = rows(lax.rem(z + 8 - d, 8) * 24, 24)
        copy(
            g2_out.at[j, source], g2_in.at[j, source], g2_s.at[j, d - 1], g2_r.at[j, d - 1], at_z(d)
        ).wait_recv()

    def g3(j, d):
        to = rows(lax.rem(x + d, 4) * 16, 16)
        return copy(g3_out.at[j, to], g3_in.at[j, rows(x * 16, 16)], g3_s.at[j, d - 1], g3_r.at[j, d - 1], at_x(d))

    def g3_wait(j, d):
        source = rows(lax.rem(x + 4 - d, 4) * 16, 16)
        copy(
            g3_out.at[j, source], g3_in.at[j, source], g3_s.at[j, d - 1], g3_r.at[j, d - 1], at_x(d)
        ).wait_recv()

    def down(j):
        span = rows(j * CF, CF)
        both = (mm(act[0], wd[0, :, span]) + mm(act[1], wd[1, :, span])).astype(BF16)
        down_out[j] = both.reshape(2, 192, CF)
        copies = f1(j)
        copies[0].start()
        copies[1].start()

    def return_z(j):
        total = sum_near(j)
        g2_out[j] = (mm(unpack_ref[0], total[:, :HF]) + mm(unpack_ref[1], total[:, HF:])).astype(BF16)
        for d in (4, 3, 5, 2, 6, 1, 7):
            g2(j, d).start()
        g2_in[j, rows(z * 24, 24)] = g2_out[j, rows(z * 24, 24)]

    def return_x(j):
        for d in range(1, 8):
            g2_wait(j, d)
        total = (g2_in[j, pl.ds(0, 96)].astype(F32) + g2_in[j, pl.ds(96, 96)].astype(F32)).astype(BF16)
        g3_out[j, :, pl.ds(0, HF)] = mm(qt_ref[0], total).astype(BF16)
        g3_out[j, :, pl.ds(HF, HF)] = mm(qt_ref[1], total).astype(BF16)
        for d in (2, 1, 3):
            g3(j, d).start()
        g3_in[j, rows(x * 16, 16)] = g3_out[j, rows(x * 16, 16)]

    def combine(j):
        for d in (1, 2, 3):
            g3_wait(j, d)
        back = g3_in[j]
        out_ref[:, rows(j * CF, CF)] = (hid[:, rows(j * CF, CF)] + mm(mix_hi, back) + mm(mix_lo, back)).astype(BF16)

    def back_stage(s, skew, body):
        pl.when((s >= skew) & (s < back_chunks + skew))(lambda: body(s - skew))

    def f_step(s, _):
        back_stage(s, 0, down)
        back_stage(s, 2, sum_far)
        back_stage(s, 4, return_z)
        back_stage(s, 6, return_x)
        back_stage(s, 7, combine)
        return 0

    lax.fori_loop(0, back_chunks + 7, f_step, 0)

    @pl.loop(0, chunks)
    def _(j):
        for c in c1(j):
            c.wait_send()
        for d in (1, 2, 3):
            c2(j, d).wait_send()
            d1(j, d).wait_send()
        for d in range(1, 8):
            d2(j, d).wait_send()

    @pl.loop(0, back_chunks)
    def _(j):
        for c in f1(j):
            c.wait_send()
        for d in (1, 2, 3):
            g3(j, d).wait_send()
        for d in range(1, 8):
            g2(j, d).wait_send()

    for c in swaps + [state1, b_z()] + [state2(d) for d in (1, 2, 3)]:
        c.wait_send()
    for group in range(2):
        for side in range(2):
            b_near(group, side).wait_send()
            b_far(group, side).wait_send()
        for d in range(4):
            b_core(group, d).wait_send()

    @pl.when(zh == 0)
    def _():
        state3.wait_send()


def selections():
    q = np.zeros((2, 96, 64), np.float32)
    pack = np.zeros((2, 96, 192), np.float32)
    for half in range(2):
        for e in range(4):
            for source in range(4):
                for s in range(3):
                    q[half, e * 24 + half * 12 + source * 3 + s, source * 16 + e * 4 + s] = 1
        for source in range(8):
            for r in range(12):
                pack[half, source * 12 + r, source * 24 + half * 12 + r] = 1
    return tuple(jnp.asarray(a, BF16) for a in (q, q.transpose(0, 2, 1), pack, pack.transpose(0, 2, 1)))


def shards(
    queries,
    keys_in,
    values_in,
    log_decay,
    attn_gain,
    out_weight,
    residual,
    moe_gain,
    router,
    gate_weight,
    up_weight,
    down_weight,
    routes,
):
    length, _, span = queries.shape
    count, _, width = residual.shape
    hidden = gate_weight.shape[2]
    n, nf = width // CW, width // CF
    flat = lambda a: a.reshape(length, span)
    dma = lambda *shape: pltpu.SemaphoreType.DMA(shape)
    vmem = lambda *shape: pltpu.VMEM(shape, BF16)
    scratch = [
        vmem(length, span), vmem(2 * n, span, HW), pltpu.VMEM((2, length, HEAD), F32),
        vmem(2, 144, HEAD), vmem(2, 144, HEAD), vmem(4, 2, 144, HEAD), vmem(2, HEAD, HEAD), vmem(2, HEAD, HEAD),
        vmem(2, hidden, width), vmem(2, hidden, width), vmem(2, hidden, width),
        vmem(n, 256, CW), vmem(n, 2, 32, CW), vmem(n, 2, 64, CW), vmem(n, 64, CW), vmem(n, 3, 16, CW),
        pltpu.VMEM((16, width), F32), pltpu.VMEM((16, 128), F32), pltpu.VMEM((384, 128), F32),
        vmem(n, 64, CW), vmem(n, 64, CW), vmem(n, 96, HW), vmem(n, 192, HW), vmem(n, 2, 192, CW),
        pltpu.VMEM((16, 16), F32), pltpu.VMEM((2, 2, 384, hidden), F32), vmem(2, 384, hidden),
        vmem(nf, 2, 192, CF), vmem(nf, 2, 48, CF), vmem(nf, 2, 2, 48, CF), vmem(nf, 192, HF), vmem(nf, 192, HF),
        vmem(nf, 64, CF), vmem(nf, 64, CF),
        dma(4), dma(3), dma(3), pltpu.SemaphoreType.DMA, pltpu.SemaphoreType.DMA, dma(3), dma(3),
        pltpu.SemaphoreType.DMA, pltpu.SemaphoreType.DMA,
        dma(2, 4), dma(2, 4), pltpu.SemaphoreType.DMA, pltpu.SemaphoreType.DMA, dma(2, 2), dma(2, 2), dma(2, 2), dma(2, 2),
    ]
    for lanes in (2, 2, 3, 3, 7, 2, 2):
        scratch += [dma(n, lanes), dma(n, lanes)]
    for lanes in (2, 2, 7, 3):
        scratch += [dma(nf, lanes), dma(nf, lanes)]
    in_vmem = pl.BlockSpec(memory_space=pltpu.VMEM)
    in_hbm = pl.BlockSpec(memory_space=pl.ANY)
    mixed = pl.pallas_call(
        block_kernel,
        out_shape=jax.ShapeDtypeStruct((count, width), BF16),
        in_specs=[in_vmem] * 5 + [in_hbm] + [in_vmem] * 8 + [in_hbm] * 3,
        out_specs=in_vmem,
        scratch_shapes=scratch,
        compiler_params=pltpu.CompilerParams(collective_id=0, has_side_effects=True, vmem_limit_bytes=67043328),
    )(
        flat(queries), flat(keys_in), flat(values_in), log_decay, attn_gain.reshape(1, span),
        out_weight, residual.reshape(count, width), moe_gain.reshape(1, width), router.T, routes.reshape(count, 2).T,
        *selections(), jnp.swapaxes(gate_weight, 1, 2), jnp.swapaxes(up_weight, 1, 2), down_weight,
    )
    return mixed.reshape(residual.shape)


def solution(mesh):
    return jax.shard_map(
        shards,
        mesh=mesh,
        in_specs=(
            P("ctx", None, "ep"),
            P("ctx", None, "ep"),
            P("ctx", None, "ep"),
            P("ep", None, "ctx"),
            P("ep"),
            P("ep", "ctx"),
            P(("ctx", "ep"), None, None),
            P(),
            P(),
            P("ep", None, "ctx"),
            P("ep", None, "ctx"),
            P("ep", "ctx", None),
            P(("ctx", "ep"), None, None),
        ),
        out_specs=P(("ctx", "ep"), None, None),
        check_vma=False,
    )
```
